32 devices in a mesh: group: 4 (over z), member: 8 (over y, x, core).
Axes of the slice: x: 2, y: 2, z: 4, core: 2. Of those that a mesh axis runs over, the one named last changes fastest.
Arguments:
- doc_mantissa: bfloat16 [16384, 4096], P(('group', 'member')), may hold values from -6 to 6
- doc_exponent: int32 [16384], P(('group', 'member')), may hold values from -1 to 1
- doc_home: int32 [16384], P(('group', 'member')), may hold values from 0 to 16383, as said below
- block_cluster: int32 [4, 16], P('group'), may hold values from 0 to 7, never falling along the last dimension, each value on 1 to 3 neighbouring positions
Outputs:
- embed_sum: bfloat16 [16384, 4096], P(('group', 'member'))
- log_density: float32 [16384], P(('group', 'member'))
The draws below stay inside these ranges and needn't reach their ends.
Inputs may be any that keep to these rules, and one draw needn't show every extreme that they name: `doc_home`: device d's home slots are d * 512 to (d + 1) * 512 - 1, devices taken in the order group then member. Every slot is the home of exactly one document. The documents of one device have at most 24 home slots on any one device, and exactly 24 on some device. `block_cluster`: within a group the ids never fall along the blocks, and every cluster is a run of 1 to 3 consecutive blocks; some cluster has exactly 3 blocks.
All inputs are finite; a program needn't handle non-finite values.
Results may differ from the reference program's by a relative error of at most 0.0073.
Values may be sent and summed in bfloat16 or wider, within the bound.
No kernel may reach another device: no remote copies, remote signals or barrier semaphores. Data moves between devices by JAX's collectives and lax.ppermute only.
A program may use at most 192 MiB of HBM per device.

```python
import math
import jax
import jax.numpy as jnp
import numpy as np
from jax import lax

D = 4096
BLK = 256
SPAN = 2
NB_GROUP = 16
ROWS_DEV = 512
DOCS = 16384
CLUSTERS = 8
N_GROUP = 4


def draw_doc_home(key, part):
    device_count = DOCS // ROWS_DEV
    average = ROWS_DEV // device_count
    half_tilt = average // 2
    key_tilt, key_order, key_dest, key_source = jax.random.split(key, 4)
    pairs_count = device_count // 2
    tilt_values = jax.random.randint(key_tilt, (pairs_count,), -half_tilt, half_tilt + 1)
    tilt_values = tilt_values.at[0].set(half_tilt)
    counts = jnp.concatenate([average + tilt_values, average - tilt_values])
    counts = counts[jax.random.permutation(key_order, device_count)]
    bucket_ends = jnp.cumsum(counts)
    slot_index = jnp.arange(ROWS_DEV, dtype=jnp.int32)
    offset = jnp.sum((slot_index[:, None] >= bucket_ends[None, :]).astype(jnp.int32), axis=1)
    source = jnp.arange(device_count, dtype=jnp.int32)[:, None]
    destination = (source + offset[None, :]) % device_count
    dest_order = jax.vmap(lambda subkey: jax.random.permutation(subkey, ROWS_DEV))(jax.random.split(key_dest, device_count))
    source_order = jax.vmap(lambda subkey: jax.random.permutation(subkey, ROWS_DEV))(jax.random.split(key_source, device_count))
    dest_slot = dest_order[destination, jnp.broadcast_to(slot_index[None, :], destination.shape)]
    home_value = destination * ROWS_DEV + dest_slot
    placed = jnp.zeros((device_count, ROWS_DEV), jnp.int32).at[jnp.broadcast_to(source, source_order.shape), source_order].set(home_value)
    return placed.reshape(-1).astype(jnp.int32)


def with_ends(drawn, key, smallest, high):
    index_at = [jax.random.randint(jax.random.fold_in(key, axis), (), 0, length) for axis, length in enumerate(drawn.shape)]
    longest = drawn.shape.index(max(drawn.shape))
    next_to = index_at[:longest] + [(index_at[longest] + 1) % drawn.shape[longest]] + index_at[longest + 1:]
    return drawn.at[tuple(index_at)].set(smallest).at[tuple(next_to)].set(high)


def level_of(own_key, shape, cuts, least, largest):
    def one(axis_at, shards_of):
        heights = jax.random.uniform(jax.random.fold_in(jax.random.fold_in(own_key, 6), axis_at), (shards_of,), jnp.float32, least / len(cuts), largest / len(cuts))
        return jnp.repeat(jnp.exp(heights), shape[axis_at] // shards_of).reshape((-1,) + (1,) * (len(shape) - axis_at - 1))

    loudness = one(*cuts[0])
    for cut in cuts[1:]:
        loudness = loudness * one(*cut)
    return loudness


def length_profile(count, total, bound, slope):
    portions = [(1 << 20) // math.isqrt(grade ** slope) + 1 for grade in range(2, count + 1)]
    spare, holding = total - bound - (count - 1), [1] * (count - 1)
    while spare > 0:
        free = [i for i in range(count - 1) if holding[i] < bound]
        pool, left = sum([portions[i] for i in free]), spare
        for i in free:
            more = min(bound - holding[i], max(1, left * portions[i] // pool), spare)
            holding[i] = holding[i] + more
            spare = spare - more
    return np.array([bound] + holding)


def ragged_sizes(rng, count, total, bound, slope):
    if count == 2:
        one = jax.random.randint(rng, (), max(1, total - bound), min(bound, total - 1) + 1)
        return jnp.stack([one, total - one])
    sizes = jnp.asarray(length_profile(count, total, bound, slope), jnp.int32)
    pairs = (count - 1) // 2
    donor, receiver = sizes[1:1 + 2 * pairs:2], sizes[2:2 + 2 * pairs:2]
    slack = jnp.minimum(donor - 1, bound - receiver)
    moved = jax.random.randint(jax.random.fold_in(rng, 1), (pairs,), 0, 1 << 20) % (slack + 1)
    sizes = sizes.at[1:1 + 2 * pairs:2].set(donor - moved).at[2:2 + 2 * pairs:2].set(receiver + moved)
    return sizes[jax.random.permutation(jax.random.fold_in(rng, 2), count)]


def noise(own_key, shape, width, most, pieces=(), held_as=jnp.bfloat16):
    drawn = width * jax.random.normal(own_key, shape, jnp.float32)
    if pieces:
        drawn = drawn * level_of(own_key, shape, pieces, -0.22, 0.18)
    return jnp.clip(drawn, -most, most).astype(held_as)


def setup_inputs(seed: int = 0) -> dict:
    key_list = jax.random.split(jax.random.key(seed), 5)
    return {
        "doc_mantissa": noise(key_list[0], (DOCS, D), 1.0, 6.0, ((0, 32),)),
        "doc_exponent": with_ends(jax.random.randint(key_list[1], (DOCS,), -1, 2), jax.random.fold_in(key_list[1], 1), -1, 1).astype(jnp.int32),
        "doc_home": draw_doc_home(jax.random.fold_in(key_list[4], 71), 0),
        "block_cluster": jax.vmap(lambda own: jnp.searchsorted(jnp.cumsum(ragged_sizes(own, CLUSTERS, NB_GROUP, SPAN + 1, 0)), jnp.arange(NB_GROUP), side="right"))(jax.random.split(key_list[3], N_GROUP)).reshape((N_GROUP, NB_GROUP)).astype(jnp.int32),
    }


KERNEL_SHIFT = 4.0
EPSILON = 1e-06

def prepare(mantissa, exponent):
    widened = mantissa.astype(jnp.float32)
    values = (widened * jnp.exp2(exponent.astype(jnp.float32))[..., None]).astype(jnp.bfloat16)
    unit_rows = (widened * lax.rsqrt(lax.optimization_barrier(jnp.mean(widened * widened, axis=-1, keepdims=True)) + EPSILON)).astype(jnp.bfloat16)
    return (values, unit_rows)

def reference(doc_mantissa, doc_exponent, doc_home, block_cluster):
    home_mantissa = jnp.zeros_like(doc_mantissa).at[doc_home].set(doc_mantissa)
    home_exponent = jnp.zeros_like(doc_exponent).at[doc_home].set(doc_exponent)
    values, unit_rows = prepare(home_mantissa, home_exponent)
    groups = block_cluster.shape[0]
    per_group = block_cluster.shape[1]
    values = values.reshape(groups, per_group, BLK, D)
    unit_rows = unit_rows.reshape(groups, per_group, BLK, D)
    padding = ((0, 0), (SPAN, SPAN), (0, 0), (0, 0))
    values_pad = jnp.pad(values, padding)
    unit_pad = jnp.pad(unit_rows, padding)
    cluster_pad = jnp.pad(block_cluster, ((0, 0), (SPAN, SPAN)), constant_values=-1)
    window = 2 * SPAN + 1
    centre = lax.broadcasted_iota(jnp.int32, (window, BLK, BLK), 0) == SPAN
    same_row = lax.broadcasted_iota(jnp.int32, (window, BLK, BLK), 1) == lax.broadcasted_iota(jnp.int32, (window, BLK, BLK), 2)

    def one_block(flat_index):
        group_index = (flat_index // per_group).astype(jnp.int32)
        block_index = (flat_index % per_group).astype(jnp.int32)
        anchor = jnp.zeros((), jnp.int32)
        near_unit = lax.dynamic_slice(unit_pad, (group_index, block_index, anchor, anchor), (1, window, BLK, D))[0]
        near_values = lax.dynamic_slice(values_pad, (group_index, block_index, anchor, anchor), (1, window, BLK, D))[0]
        near_cluster = lax.dynamic_slice(cluster_pad, (group_index, block_index), (1, window))[0]
        own_cluster = near_cluster[SPAN]
        own_unit = near_unit[SPAN]
        scores = jnp.einsum('id,tjd->tij', own_unit.astype(jnp.float32), near_unit.astype(jnp.float32))
        kernel = jnp.exp(scores * D ** (-0.5) - KERNEL_SHIFT)
        kept_pairs = (near_cluster == own_cluster)[:, None, None] & jnp.logical_not(centre & same_row)
        kernel = jnp.where(kept_pairs, kernel, 0.0)
        density = lax.optimization_barrier(jnp.sum(kernel, axis=(0, 2)))
        kernel_half = lax.optimization_barrier(kernel.astype(jnp.bfloat16))
        summed = jnp.einsum('tij,tjd->id', kernel_half.astype(jnp.float32), near_values.astype(jnp.float32))
        return (summed.astype(jnp.bfloat16), jnp.log(density))
    summed, log_values = lax.map(one_block, jnp.arange(groups * per_group, dtype=jnp.int32))
    return (summed.reshape(-1, D), log_values.reshape(-1))
```

```python
import jax
import jax.numpy as jnp
from jax import lax
from jax.experimental import pallas as pl
from jax.experimental.pallas import tpu as pltpu
from jax.sharding import PartitionSpec as P

BLK = 256
B_DEV = 2
SPAN = 2
RUN = SPAN + 1
WINDOW = B_DEV + 2 * SPAN
META = 128
KERNEL_SHIFT = 4.0
EPSILON = 1e-06
CHUNKS = (2048, 2048)
PIECE = 512

F32 = jnp.float32
BF16 = jnp.bfloat16
VM = pl.BlockSpec(memory_space=pltpu.VMEM)
SM = pl.BlockSpec(memory_space=pltpu.SMEM)
HBM = pl.BlockSpec(memory_space=pltpu.HBM)
WHOLE = pltpu.CompilerParams(vmem_limit_bytes=64 * 1024 * 1024)


def halfway(width):
    return max(PIECE, (width // 2) // PIECE * PIECE)


def steps(width):
    cut = halfway(width)
    return [
        (at, min(PIECE, end - at))
        for begin, end in ((0, cut), (cut, width))
        for at in range(begin, end, PIECE)
    ]


def relayed(members):
    return members == 8


def column_of(row):
    return jnp.broadcast_to(row, (128, row.shape[1])).T[:, 0:1]


def row_of(column):
    return jnp.broadcast_to(column, (column.shape[0], 128)).T[0:1]


def pack(doc, guide, offset, width, devices, capacity):
    rows, features = doc.shape
    slots = devices * capacity
    first = isinstance(guide, tuple)
    tail = META if first else 0
    pieces = steps(width)
    rest = [(at, min(PIECE, features - at)) for at in range(width, features, PIECE)] if first else []
    count = len(pieces)

    def kernel(*refs):
        if first:
            home_ref, exponent_ref, doc_ref, out_ref, order_ref, tile, packed, sems = refs
        else:
            order_ref, doc_ref, out_ref, tile, packed, sems = refs
        loads, stores = [], []
        for p, (at, wide) in enumerate(pieces + rest):
            loads.append(
                pltpu.make_async_copy(
                    doc_ref.at[:, pl.ds(offset + at, wide)], tile.at[:, pl.ds(at, wide)], sems.at[p]
                )
            )
            loads[-1].start()

        def send(begin, end):
            piece = pl.ds(begin, end - begin)
            stores.append(
                pltpu.make_async_copy(
                    packed.at[:, piece], out_ref.at[:, piece], sems.at[len(loads) + len(stores)]
                )
            )
            stores[-1].start()

        if first:
            home = home_ref[...].astype(F32)
            target = jnp.floor((home + 0.5) * (1.0 / rows))
            target_col = column_of(target)
            earlier = lax.broadcasted_iota(jnp.int32, (rows, rows), 0) < lax.broadcasted_iota(
                jnp.int32, (rows, rows), 1
            )
            rank = jnp.sum(
                jnp.where(earlier & (target_col == target), 1.0, 0.0), axis=0, keepdims=True
            )
            position = (target * capacity + rank).astype(jnp.int32)
            order = jnp.where(
                lax.broadcasted_iota(jnp.int32, (slots, rows), 0) == position, 1.0, 0.0
            ).astype(BF16)
            order_ref[...] = order
        else:
            order = order_ref[...]
        for p, (at, wide) in enumerate(pieces):
            loads[p].wait()
            packed[:, at : at + wide] = jnp.dot(
                order, tile[:, at : at + wide], preferred_element_type=F32
            ).astype(BF16)
            send(at, at + wide)
        if first:
            for load in loads[count:]:
                load.wait()
            total = jnp.zeros((rows, 128), F32)
            for at in range(0, features, 128):
                values = tile[:, at : at + 128].astype(F32)
                total = total + values * values
            square = row_of(jnp.sum(total, axis=1, keepdims=True))
            inverse = lax.rsqrt(square * (1.0 / features) + EPSILON)
            high = inverse.astype(BF16).astype(F32)
            middle = (inverse - high).astype(BF16).astype(F32)
            slot = home - target * rows
            slot_high = jnp.floor((slot + 0.5) * (1.0 / 32))
            field = lax.broadcasted_iota(jnp.int32, (META, rows), 0)
            meta = jnp.where(field == 0, 1.0, 0.0)
            for f, value in enumerate(
                (
                    slot_high,
                    slot - slot_high * 32,
                    exponent_ref[...].astype(F32),
                    high,
                    middle,
                    inverse - high - middle,
                ),
                1,
            ):
                meta = jnp.where(field == f, value, meta)
            packed[:, width:] = lax.dot_general(
                order, meta.astype(BF16), (((1,), (1,)), ((), ())), preferred_element_type=F32
            ).astype(BF16)
            send(width, width + META)
        for copy in stores:
            copy.wait()

    sent = jax.ShapeDtypeStruct((slots, width + tail), BF16)
    return pl.pallas_call(
        kernel,
        in_specs=[VM, VM, HBM] if first else [VM, HBM],
        out_specs=(HBM, VM) if first else HBM,
        out_shape=(sent, jax.ShapeDtypeStruct((slots, rows), BF16)) if first else sent,
        scratch_shapes=[
            pltpu.VMEM((rows, features if first else width), BF16),
            pltpu.VMEM((slots, width + tail), BF16),
            pltpu.SemaphoreType.DMA((2 * count + len(rest) + 1,)),
        ],
        compiler_params=WHOLE,
        name="pack_first" if first else "pack_next",
    )(*(guide if first else (guide,)), doc)


def unpack(got, order, rows, halves):
    slots, width = got.shape
    first = order is None
    pieces = steps(width)
    count = len(pieces)
    cut = halfway(width)

    def kernel(*refs):
        got_ref = refs[0]
        outs = 1 if first else 2
        out_refs = refs[outs : outs + 1 + 2 * halves]
        if first:
            order_ref, tile, placed, sems = refs[outs + 1 + 2 * halves :]
        else:
            order_ref = refs[1]
            tile, placed, sems = refs[outs + 1 + 2 * halves :]
        loads, stores = [], []
        for p in ([count - 1] if first else []) + list(range(count - 1 if first else count)):
            at, wide = pieces[p]
            piece = pl.ds(at, wide)
            loads.append((p, pltpu.make_async_copy(got_ref.at[:, piece], tile.at[:, piece], sems.at[p])))
            loads[-1][1].start()
        if first:
            loads[0][1].wait()
            fields = tile[:, width - META :].astype(F32)
            slot = fields[:, 1:2] * 32 + fields[:, 2:3]
            home = lax.broadcasted_iota(jnp.int32, (slots, rows), 1).astype(F32)
            hit = (home == slot) & (fields[:, 0:1] > 0.5)
            order = jnp.where(hit, 1.0, 0.0).T.astype(BF16)
            order_ref[...] = order
        else:
            order = order_ref[...]
        for number, (p, load) in enumerate(loads):
            at, wide = pieces[p]
            if number > 0 or not first:
                load.wait()
            placed[:, at : at + wide] = jnp.dot(
                order, tile[:, at : at + wide], preferred_element_type=F32
            ).astype(BF16)
            source = placed.at[:, pl.ds(at, wide)]
            targets = [out_refs[0].at[:, pl.ds(at, wide)]]
            if halves:
                half, inner = (1, at) if at < cut else (2, at - cut)
                targets.append(out_refs[half].at[:, pl.ds(inner, wide)])
            for target in targets:
                stores.append(pltpu.make_async_copy(source, target, sems.at[count + len(stores)]))
                stores[-1].start()
        for copy in stores:
            copy.wait()

    outs = [jax.ShapeDtypeStruct((rows, width), BF16)]
    if halves:
        outs += [
            jax.ShapeDtypeStruct((rows, cut), BF16),
            jax.ShapeDtypeStruct((rows, width - cut), BF16),
        ]
    if first:
        outs.append(jax.ShapeDtypeStruct((rows, slots), BF16))
    result = pl.pallas_call(
        kernel,
        in_specs=[HBM] if first else [HBM, VM],
        out_specs=[HBM] * (1 + 2 * halves) + [VM] * first,
        out_shape=outs,
        scratch_shapes=[
            pltpu.VMEM(got.shape, BF16),
            pltpu.VMEM((rows, width), BF16),
            pltpu.SemaphoreType.DMA((3 * count,)),
        ],
        compiler_params=WHOLE,
        name="unpack_first" if first else "unpack_next",
    )(*((got,) if first else (got, order)))
    return (result[:-1], result[-1]) if first else (result, order)


def runs(member_ref, cluster_ref):
    blocks = cluster_ref.shape[1]
    base = member_ref[0] * B_DEV

    def cluster(index):
        inside = (index >= 0) & (index < blocks)
        return jnp.where(inside, cluster_ref[0, jnp.clip(index, 0, blocks - 1)], -1)

    result = []
    for b in range(B_DEV):
        mine = cluster(base + b)
        back = jnp.where(
            cluster(base + b - 2) == mine, 2, jnp.where(cluster(base + b - 1) == mine, 1, 0)
        )
        links = [
            jnp.where(cluster(base + b - back + k) == mine, 1, 0) for k in range(RUN)
        ]
        result.append((back, links))
    return result


def load_window(member_ref, members, parts, window, sems, column):
    rows, width = parts[1].shape
    cut = halfway(width)
    middle = members // 2
    groups = []
    for at, wide in steps(width):
        group = []
        for side, ref in enumerate(parts[:3]):
            target = window.at[pl.ds(side * rows, rows), pl.ds(column + at, wide)]
            sem = sems.at[len(groups), side]
            plain = pltpu.make_async_copy(ref.at[:, pl.ds(at, wide)], target, sem)
            group.append(plain)
            if side == 1 or len(parts) == 3:
                plain.start()
                continue
            half, inner = (parts[3], at) if at < cut else (parts[4], at - cut)
            other = pltpu.make_async_copy(half.at[:, pl.ds(inner, wide)], target, sem)
            crossed = member_ref[0] == (middle if side == 0 else middle - 1)
            pl.when(crossed)(other.start)
            pl.when(jnp.logical_not(crossed))(plain.start)
        groups.append((column + at, wide, group))
    return groups


def run_scores(window, back, b, column, width):
    first = pl.multiple_of((SPAN + b - back) * BLK, BLK)
    return lax.dot_general(
        window[(SPAN + b) * BLK : (SPAN + b + 1) * BLK, column : column + width],
        window[pl.ds(first, RUN * BLK), column : column + width],
        (((1,), (1,)), ((), ())),
        preferred_element_type=F32,
    )


def partial_scores(member, members, cluster, parts, score):
    rows, width = parts[1].shape
    given = score is not None
    number = len(parts)

    def kernel(member_ref, cluster_ref, *refs):
        if given:
            score_in, score_ref, window, sems = refs[number:]
        else:
            score_ref, factor_ref, window, sems = refs[number:]
        found = runs(member_ref, cluster_ref)
        groups = load_window(member_ref, members, refs[:number], window, sems, 0)
        for p, (column, wide, group) in enumerate(groups):
            for copy in group:
                copy.wait()
            if not given:
                wide = min(wide, width - META - column)
            if wide == 0:
                continue
            for b in range(B_DEV):
                value = run_scores(window, found[b][0], b, column, wide)
                if p > 0:
                    value = value + score_ref[b]
                elif given:
                    value = value + score_in[b]
                score_ref[b] = value
        if not given:
            for side in range(3):
                fields = window[side * rows : (side + 1) * rows, width - META :].astype(F32).T
                field = lax.broadcasted_iota(jnp.int32, (8, rows), 0)
                inverse = fields[4:5] + fields[5:6] + fields[6:7]
                factor_ref[side] = jnp.where(field == 0, inverse, jnp.exp2(fields[3:4]))

    score_shape = jax.ShapeDtypeStruct((B_DEV, BLK, RUN * BLK), F32)
    return pl.pallas_call(
        kernel,
        in_specs=[SM, SM] + [HBM] * number + [VM] * given,
        out_shape=score_shape if given else (score_shape, jax.ShapeDtypeStruct((3, 8, rows), F32)),
        scratch_shapes=[
            pltpu.VMEM((3 * rows, width), BF16),
            pltpu.SemaphoreType.DMA((len(steps(width)), 3)),
        ],
        compiler_params=WHOLE,
        name="partial_scores",
    )(member, cluster, *parts, *([score] if given else []))


def finish(member, members, cluster, chunks, score, factor, features):
    rows = chunks[0][1].shape[0]
    count = len(chunks)
    widths = [chunk[1].shape[1] for chunk in chunks]
    pieces = [len(steps(width)) for width in widths]
    number = len(chunks[0])
    last = count - 1

    def kernel(member_ref, cluster_ref, *refs):
        parts = [refs[number * c : number * (c + 1)] for c in range(count)]
        score_in, factor_in, out_ref, log_ref = refs[number * count : number * count + 4]
        window, packed, value_ref, factor_ref, early_sems, out_sems = refs[
            number * count + 4 : number * count + 10
        ]
        load_sems = refs[number * count + 10 :]
        found = runs(member_ref, cluster_ref)
        loads = {}

        def load(c):
            loads[c] = load_window(
                member_ref, members, parts[c], window, load_sems[c], sum(widths[:c])
            )

        load(last)
        early = [
            pltpu.make_async_copy(score_in, value_ref, early_sems.at[0]),
            pltpu.make_async_copy(factor_in, factor_ref, early_sems.at[1]),
        ]
        for copy in early:
            copy.start()
        for c in range(last):
            load(c)
        for copy in early:
            copy.wait()
        for column, wide, group in loads[last]:
            for copy in group:
                copy.wait()
            for b in range(B_DEV):
                value_ref[b] += run_scores(window, found[b][0], b, column, wide)
        apart = lax.broadcasted_iota(jnp.int32, (BLK, BLK), 0) - lax.broadcasted_iota(
            jnp.int32, (BLK, BLK), 1
        )
        weights = []
        for b in range(B_DEV):
            back, links = found[b]
            mine = factor_ref[1, :, b * BLK : (b + 1) * BLK]
            row_scale = column_of(mine[0:1]) * features**-0.5
            density = jnp.zeros((BLK, 1), F32)
            tiles = []
            for k in range(RUN):
                block = SPAN + b - back + k
                far = factor_ref[block // B_DEV, :, pl.ds(pl.multiple_of((block % B_DEV) * BLK, BLK), BLK)]
                value = jnp.exp(
                    value_ref[b, :, k * BLK : (k + 1) * BLK] * row_scale * far[0:1] - KERNEL_SHIFT
                )
                kept = (apart + jnp.where(back == k, 0, 2 * BLK) != 0) & (
                    jnp.full((BLK, BLK), links[k], jnp.int32) > 0
                )
                value = jnp.where(kept, value, 0.0)
                density = density + jnp.sum(value, axis=1, keepdims=True)
                tiles.append((value.astype(BF16).astype(F32) * far[1:2]).astype(BF16))
            weights.append(jnp.concatenate(tiles, axis=1))
            log_ref[:, b * BLK : (b + 1) * BLK] = jnp.log(row_of(density))
        outgoing = []
        for c in [last] + list(range(last)):
            for column, wide, group in loads[c]:
                if c != last:
                    for copy in group:
                        copy.wait()
                if c == 0:
                    wide = min(wide, widths[0] - META - column)
                    if wide == 0:
                        continue
                out_at = column if c == 0 else column - META
                for b in range(B_DEV):
                    first = pl.multiple_of((SPAN + b - found[b][0]) * BLK, BLK)
                    packed[b * BLK : (b + 1) * BLK, out_at : out_at + wide] = jnp.dot(
                        weights[b],
                        window[pl.ds(first, RUN * BLK), column : column + wide],
                        preferred_element_type=F32,
                    ).astype(BF16)
                piece = pl.ds(out_at, wide)
                copy = pltpu.make_async_copy(
                    packed.at[:, piece], out_ref.at[:, piece], out_sems.at[len(outgoing)]
                )
                copy.start()
                outgoing.append(copy)
        for copy in outgoing:
            copy.wait()

    flat = [ref for chunk in chunks for ref in chunk]
    return pl.pallas_call(
        kernel,
        in_specs=[SM, SM] + [HBM] * (len(flat) + 2),
        out_specs=(HBM, VM),
        out_shape=(
            jax.ShapeDtypeStruct((rows, features), BF16),
            jax.ShapeDtypeStruct((1, rows), F32),
        ),
        scratch_shapes=[
            pltpu.VMEM((3 * rows, features + META), BF16),
            pltpu.VMEM((rows, features), BF16),
            pltpu.VMEM((B_DEV, BLK, RUN * BLK), F32),
            pltpu.VMEM((3, 8, rows), F32),
            pltpu.SemaphoreType.DMA((2,)),
            pltpu.SemaphoreType.DMA((sum(pieces),)),
        ]
        + [pltpu.SemaphoreType.DMA((pieces_of, 3)) for pieces_of in pieces],
        compiler_params=WHOLE,
        name="finish",
    )(member, cluster, *flat, score, factor)


def neighbours(own, members):
    middle = members // 2
    broken = middle if relayed(members) else 0
    if broken:
        over = lax.ppermute(own[2], "member", [(middle - 1, members - 1), (middle, 0)])
        straight = lax.ppermute(own[1], "member", [(middle - 1, middle), (middle, middle - 1)])
    left = lax.ppermute(own[0], "member", [(i - 1, i) for i in range(1, members) if i != broken])
    right = lax.ppermute(own[0], "member", [(i, i - 1) for i in range(1, members) if i != broken])
    if not broken:
        return (left, own[0], right)
    around = lax.ppermute(over, "member", [(members - 1, middle), (0, middle - 1)])
    return (left, own[0], right, straight, around)


def body(doc_mantissa, doc_exponent, doc_home, block_cluster):
    rows, features = doc_mantissa.shape
    members = lax.axis_size("member")
    devices = lax.axis_size("group") * members
    capacity = rows // devices * 3 // 2
    member = lax.axis_index("member").reshape(1)
    sends = []
    guide = (doc_home[None, :], doc_exponent[None, :])
    for c, width in enumerate(CHUNKS):
        sent = pack(doc_mantissa, guide, sum(CHUNKS[:c]), width, devices, capacity)
        if c == 0:
            sent, guide = sent
        sends.append(sent)

    chunks = []
    order = score = None
    for c in range(len(CHUNKS)):
        got = lax.all_to_all(
            sends[c].reshape(devices, capacity, -1), ("group", "member"), 0, 0, tiled=True
        ).reshape(devices * capacity, -1)
        if c > 0:
            got, score = lax.optimization_barrier((got, score))
        own, order = unpack(got, order, rows, relayed(members))
        chunks.append(neighbours(own, members))
        if c + 1 < len(CHUNKS):
            score = partial_scores(member, members, block_cluster, chunks[c], score)
            if c == 0:
                score, factor = score
    embed_sum, log_density = finish(
        member, members, block_cluster, chunks, score, factor, features
    )
    return embed_sum, log_density.reshape(rows)


def solution(mesh):
    return jax.shard_map(
        body,
        mesh=mesh,
        in_specs=(
            P(("group", "member"), None),
            P(("group", "member")),
            P(("group", "member")),
            P("group", None),
        ),
        out_specs=(P(("group", "member"), None), P(("group", "member"))),
        check_vma=False,
    )
```

```python
import jax
import jax.numpy as jnp
from jax import lax
from jax.experimental import pallas as pl
from jax.experimental.pallas import tpu as pltpu
from jax.sharding import PartitionSpec as P

BLK = 256
B_DEV = 2
SPAN = 2
RUN = SPAN + 1
WINDOW = B_DEV + 2 * SPAN
META = 128
KERNEL_SHIFT = 4.0
EPSILON = 1e-06
CHUNKS = (1920, 2176)
PIECE = 512

F32 = jnp.float32
BF16 = jnp.bfloat16
VM = pl.BlockSpec(memory_space=pltpu.VMEM)
SM = pl.BlockSpec(memory_space=pltpu.SMEM)
HBM = pl.BlockSpec(memory_space=pltpu.HBM)
WHOLE = pltpu.CompilerParams(vmem_limit_bytes=64 * 1024 * 1024)


def halfway(width):
    return (width // 2) // BLK * BLK


def steps(width):
    cut = halfway(width)
    return [
        (at, min(PIECE, end - at))
        for begin, end in ((0, cut), (cut, width))
        for at in range(begin, end, PIECE)
    ]


def relayed(members):
    return members == 8


def column_of(row):
    return jnp.broadcast_to(row, (128, row.shape[1])).T[:, 0:1]


def row_of(column):
    return jnp.broadcast_to(column, (column.shape[0], 128)).T[0:1]


def pack(doc, guide, offset, width, devices, capacity):
    rows, features = doc.shape
    slots = devices * capacity
    first = isinstance(guide, tuple)
    tail = META if first else 0
    pieces = steps(width)
    rest = [(at, min(PIECE, features - at)) for at in range(width, features, PIECE)] if first else []
    count = len(pieces)

    def kernel(*refs):
        if first:
            home_ref, exponent_ref, doc_ref, out_ref, order_ref, tile, packed, sems = refs
        else:
            order_ref, doc_ref, out_ref, tile, packed, sems = refs
        loads, stores = [], []
        for p, (at, wide) in enumerate(pieces + rest):
            loads.append(
                pltpu.make_async_copy(
                    doc_ref.at[:, pl.ds(offset + at, wide)], tile.at[:, pl.ds(at, wide)], sems.at[p]
                )
            )
            loads[-1].start()

        def send(begin, end):
            piece = pl.ds(begin, end - begin)
            stores.append(
                pltpu.make_async_copy(
                    packed.at[:, piece], out_ref.at[:, piece], sems.at[len(loads) + len(stores)]
                )
            )
            stores[-1].start()

        if first:
            home = home_ref[...].astype(F32)
            target = jnp.floor((home + 0.5) * (1.0 / rows))
            target_col = column_of(target)
            earlier = lax.broadcasted_iota(jnp.int32, (rows, rows), 0) < lax.broadcasted_iota(
                jnp.int32, (rows, rows), 1
            )
            rank = jnp.sum(
                jnp.where(earlier & (target_col == target), 1.0, 0.0), axis=0, keepdims=True
            )
            position = (target * capacity + rank).astype(jnp.int32)
            order = jnp.where(
                lax.broadcasted_iota(jnp.int32, (slots, rows), 0) == position, 1.0, 0.0
            ).astype(BF16)
            order_ref[...] = order
        else:
            order = order_ref[...]
        for p, (at, wide) in enumerate(pieces):
            loads[p].wait()
            packed[:, at : at + wide] = jnp.dot(
                order, tile[:, at : at + wide], preferred_element_type=F32
            ).astype(BF16)
            send(at, at + wide)
        if first:
            for load in loads[count:]:
                load.wait()
            total = jnp.zeros((rows, 128), F32)
            for at in range(0, features, 128):
                values = tile[:, at : at + 128].astype(F32)
                total = total + values * values
            square = row_of(jnp.sum(total, axis=1, keepdims=True))
            inverse = lax.rsqrt(square * (1.0 / features) + EPSILON)
            high = inverse.astype(BF16).astype(F32)
            middle = (inverse - high).astype(BF16).astype(F32)
            slot = home - target * rows
            slot_high = jnp.floor((slot + 0.5) * (1.0 / 32))
            field = lax.broadcasted_iota(jnp.int32, (META, rows), 0)
            meta = jnp.where(field == 0, 1.0, 0.0)
            for f, value in enumerate(
                (
                    slot_high,
                    slot - slot_high * 32,
                    exponent_ref[...].astype(F32),
                    high,
                    middle,
                    inverse - high - middle,
                ),
                1,
            ):
                meta = jnp.where(field == f, value, meta)
            packed[:, width:] = lax.dot_general(
                order, meta.astype(BF16), (((1,), (1,)), ((), ())), preferred_element_type=F32
            ).astype(BF16)
            send(width, width + META)
        for copy in stores:
            copy.wait()

    sent = jax.ShapeDtypeStruct((slots, width + tail), BF16)
    return pl.pallas_call(
        kernel,
        in_specs=[VM, VM, HBM] if first else [VM, HBM],
        out_specs=(HBM, VM) if first else HBM,
        out_shape=(sent, jax.ShapeDtypeStruct((slots, rows), BF16)) if first else sent,
        scratch_shapes=[
            pltpu.VMEM((rows, features if first else width), BF16),
            pltpu.VMEM((slots, width + tail), BF16),
            pltpu.SemaphoreType.DMA((2 * count + len(rest) + 1,)),
        ],
        compiler_params=WHOLE,
        name="pack_first" if first else "pack_next",
    )(*(guide if first else (guide,)), doc)


def unpack(got, order, rows):
    slots, width = got.shape
    first = order is None
    pieces = steps(width)
    count = len(pieces)
    cut = halfway(width)

    def kernel(*refs):
        got_ref = refs[0]
        outs = 1 if first else 2
        out_refs = refs[outs : outs + 3]
        if first:
            order_ref, tile, placed, sems = refs[outs + 3 :]
        else:
            order_ref = refs[1]
            tile, placed, sems = refs[outs + 3 :]
        loads, stores = [], []
        for p in ([count - 1] if first else []) + list(range(count - 1 if first else count)):
            at, wide = pieces[p]
            piece = pl.ds(at, wide)
            loads.append((p, pltpu.make_async_copy(got_ref.at[:, piece], tile.at[:, piece], sems.at[p])))
            loads[-1][1].start()
        if first:
            loads[0][1].wait()
            fields = tile[:, width - META :].astype(F32)
            slot = fields[:, 1:2] * 32 + fields[:, 2:3]
            home = lax.broadcasted_iota(jnp.int32, (slots, rows), 1).astype(F32)
            hit = (home == slot) & (fields[:, 0:1] > 0.5)
            order = jnp.where(hit, 1.0, 0.0).T.astype(BF16)
            order_ref[...] = order
        else:
            order = order_ref[...]
        for number, (p, load) in enumerate(loads):
            at, wide = pieces[p]
            if number > 0 or not first:
                load.wait()
            placed[:, at : at + wide] = jnp.dot(
                order, tile[:, at : at + wide], preferred_element_type=F32
            ).astype(BF16)
            source = placed.at[:, pl.ds(at, wide)]
            half, inner = (1, at) if at < cut else (2, at - cut)
            for target in (
                out_refs[half].at[:, pl.ds(inner, wide)],
                out_refs[0].at[:, pl.ds(at, wide)],
            ):
                stores.append(pltpu.make_async_copy(source, target, sems.at[count + len(stores)]))
                stores[-1].start()
        for copy in stores:
            copy.wait()

    outs = [jax.ShapeDtypeStruct((rows, columns), BF16) for columns in (width, cut, width - cut)]
    if first:
        outs.append(jax.ShapeDtypeStruct((rows, slots), BF16))
    result = pl.pallas_call(
        kernel,
        in_specs=[HBM] if first else [HBM, VM],
        out_specs=[HBM] * 3 + [VM] * first,
        out_shape=outs,
        scratch_shapes=[
            pltpu.VMEM(got.shape, BF16),
            pltpu.VMEM((rows, width), BF16),
            pltpu.SemaphoreType.DMA((3 * count,)),
        ],
        compiler_params=WHOLE,
        name="unpack_first" if first else "unpack_next",
    )(*((got,) if first else (got, order)))
    return result[:3], result[3] if first else order


def runs(member_ref, cluster_ref):
    blocks = cluster_ref.shape[1]
    base = member_ref[0] * B_DEV

    def cluster(index):
        inside = (index >= 0) & (index < blocks)
        return jnp.where(inside, cluster_ref[0, jnp.clip(index, 0, blocks - 1)], -1)

    result = []
    for b in range(B_DEV):
        mine = cluster(base + b)
        back = jnp.where(
            cluster(base + b - 2) == mine, 2, jnp.where(cluster(base + b - 1) == mine, 1, 0)
        )
        links = [
            jnp.where(cluster(base + b - back + k) == mine, 1, 0) for k in range(RUN)
        ]
        result.append((back, links))
    return result


def load_window(member_ref, members, parts, window, sems, column):
    own, partner, near, far = parts[:4]
    rows, width = own.shape
    cut = halfway(width)
    member = member_ref[0]
    partner_at = pl.multiple_of((1 - member % 2) * 2 * rows, rows)
    other_at = pl.multiple_of((member % 2) * 2 * rows, rows)
    middle = (member == members // 2) | (member == members // 2 - 1)
    groups = []
    for at, wide in steps(width):
        piece = pl.ds(at, wide)
        target = pl.ds(column + at, wide)
        half, inner = (near, at) if at < cut else (far, at - cut)
        group = [
            pltpu.make_async_copy(source, window.at[pl.ds(begin, rows), target], sems.at[len(groups), n])
            for n, (source, begin) in enumerate(
                (
                    (own.at[:, piece], rows),
                    (partner.at[:, piece], partner_at),
                    (half.at[:, pl.ds(inner, wide)], other_at),
                )
            )
        ]
        group[0].start()
        group[1].start()
        if at < cut or len(parts) == 4:
            group[2].start()
        else:
            relay = pltpu.make_async_copy(
                parts[4].at[:, pl.ds(inner, wide)],
                window.at[pl.ds(other_at, rows), target],
                sems.at[len(groups), 2],
            )
            pl.when(middle)(relay.start)
            pl.when(jnp.logical_not(middle))(group[2].start)
        groups.append((column + at, wide, group))
    return groups


def run_scores(window, back, b, column, width):
    first = pl.multiple_of((SPAN + b - back) * BLK, BLK)
    return lax.dot_general(
        window[(SPAN + b) * BLK : (SPAN + b + 1) * BLK, column : column + width],
        window[pl.ds(first, RUN * BLK), column : column + width],
        (((1,), (1,)), ((), ())),
        preferred_element_type=F32,
    )


def partial_scores(member, members, cluster, parts, score):
    rows, width = parts[0].shape
    given = score is not None
    number = len(parts)

    def kernel(member_ref, cluster_ref, *refs):
        if given:
            score_in, score_ref, window, sems = refs[number:]
        else:
            score_ref, factor_ref, window, sems = refs[number:]
        found = runs(member_ref, cluster_ref)
        groups = load_window(member_ref, members, refs[:number], window, sems, 0)
        for p, (column, wide, group) in enumerate(groups):
            for copy in group:
                copy.wait()
            if not given:
                wide = min(wide, width - META - column)
            if wide == 0:
                continue
            for b in range(B_DEV):
                value = run_scores(window, found[b][0], b, column, wide)
                if p > 0:
                    value = value + score_ref[b]
                elif given:
                    value = value + score_in[b]
                score_ref[b] = value
        if not given:
            for side in range(3):
                fields = window[side * rows : (side + 1) * rows, width - META :].astype(F32).T
                field = lax.broadcasted_iota(jnp.int32, (8, rows), 0)
                inverse = fields[4:5] + fields[5:6] + fields[6:7]
                factor_ref[side] = jnp.where(field == 0, inverse, jnp.exp2(fields[3:4]))

    score_shape = jax.ShapeDtypeStruct((B_DEV, BLK, RUN * BLK), F32)
    return pl.pallas_call(
        kernel,
        in_specs=[SM, SM] + [HBM] * number + [VM] * given,
        out_shape=score_shape if given else (score_shape, jax.ShapeDtypeStruct((3, 8, rows), F32)),
        scratch_shapes=[
            pltpu.VMEM((3 * rows, width), BF16),
            pltpu.SemaphoreType.DMA((len(steps(width)), 3)),
        ],
        compiler_params=WHOLE,
        name="partial_scores",
    )(member, cluster, *parts, *([score] if given else []))


def finish(member, members, cluster, chunks, score, factor, features):
    rows = chunks[0][0].shape[0]
    count = len(chunks)
    widths = [chunk[0].shape[1] for chunk in chunks]
    pieces = [len(steps(width)) for width in widths]
    number = len(chunks[0])
    last = count - 1

    def kernel(member_ref, cluster_ref, *refs):
        parts = [refs[number * c : number * (c + 1)] for c in range(count)]
        score_in, factor_in, out_ref, log_ref = refs[number * count : number * count + 4]
        window, packed, value_ref, factor_ref, early_sems, out_sems = refs[
            number * count + 4 : number * count + 10
        ]
        load_sems = refs[number * count + 10 :]
        found = runs(member_ref, cluster_ref)
        loads = {}

        def load(c):
            loads[c] = load_window(
                member_ref, members, parts[c], window, load_sems[c], sum(widths[:c])
            )

        load(last)
        early = [
            pltpu.make_async_copy(score_in, value_ref, early_sems.at[0]),
            pltpu.make_async_copy(factor_in, factor_ref, early_sems.at[1]),
        ]
        for copy in early:
            copy.start()
        for c in range(last):
            load(c)
        for copy in early:
            copy.wait()
        for column, wide, group in loads[last]:
            for copy in group:
                copy.wait()
            for b in range(B_DEV):
                value_ref[b] += run_scores(window, found[b][0], b, column, wide)
        apart = lax.broadcasted_iota(jnp.int32, (BLK, BLK), 0) - lax.broadcasted_iota(
            jnp.int32, (BLK, BLK), 1
        )
        weights = []
        for b in range(B_DEV):
            back, links = found[b]
            mine = factor_ref[1, :, b * BLK : (b + 1) * BLK]
            row_scale = column_of(mine[0:1]) * features**-0.5
            density = jnp.zeros((BLK, 1), F32)
            tiles = []
            for k in range(RUN):
                block = SPAN + b - back + k
                far = factor_ref[block // B_DEV, :, pl.ds(pl.multiple_of((block % B_DEV) * BLK, BLK), BLK)]
                value = jnp.exp(
                    value_ref[b, :, k * BLK : (k + 1) * BLK] * row_scale * far[0:1] - KERNEL_SHIFT
                )
                kept = (apart + jnp.where(back == k, 0, 2 * BLK) != 0) & (
                    jnp.full((BLK, BLK), links[k], jnp.int32) > 0
                )
                value = jnp.where(kept, value, 0.0)
                density = density + jnp.sum(value, axis=1, keepdims=True)
                tiles.append((value.astype(BF16).astype(F32) * far[1:2]).astype(BF16))
            weights.append(jnp.concatenate(tiles, axis=1))
            log_ref[:, b * BLK : (b + 1) * BLK] = jnp.log(row_of(density))
        outgoing = []
        for c in [last] + list(range(last)):
            for column, wide, group in loads[c]:
                if c != last:
                    for copy in group:
                        copy.wait()
                if c == 0:
                    wide = min(wide, widths[0] - META - column)
                    if wide == 0:
                        continue
                out_at = column if c == 0 else column - META
                for b in range(B_DEV):
                    first = pl.multiple_of((SPAN + b - found[b][0]) * BLK, BLK)
                    packed[b * BLK : (b + 1) * BLK, out_at : out_at + wide] = jnp.dot(
                        weights[b],
                        window[pl.ds(first, RUN * BLK), column : column + wide],
                        preferred_element_type=F32,
                    ).astype(BF16)
                piece = pl.ds(out_at, wide)
                copy = pltpu.make_async_copy(
                    packed.at[:, piece], out_ref.at[:, piece], out_sems.at[len(outgoing)]
                )
                copy.start()
                outgoing.append(copy)
        for copy in outgoing:
            copy.wait()

    flat = [ref for chunk in chunks for ref in chunk]
    return pl.pallas_call(
        kernel,
        in_specs=[SM, SM] + [HBM] * (len(flat) + 2),
        out_specs=(HBM, VM),
        out_shape=(
            jax.ShapeDtypeStruct((rows, features), BF16),
            jax.ShapeDtypeStruct((1, rows), F32),
        ),
        scratch_shapes=[
            pltpu.VMEM((3 * rows, features + META), BF16),
            pltpu.VMEM((rows, features), BF16),
            pltpu.VMEM((B_DEV, BLK, RUN * BLK), F32),
            pltpu.VMEM((3, 8, rows), F32),
            pltpu.SemaphoreType.DMA((2,)),
            pltpu.SemaphoreType.DMA((sum(pieces),)),
        ]
        + [pltpu.SemaphoreType.DMA((pieces_of, 3)) for pieces_of in pieces],
        compiler_params=WHOLE,
        name="finish",
    )(member, cluster, *flat, score, factor)


def neighbours(own, near, far, members):
    middle = members // 2
    odd = range(1, members - 1, 2)
    hops = [(i, i + 1) for i in odd] + [(i + 1, i) for i in odd]
    around = [(middle - 1, members - 1), (middle, 0)]
    onward = [(members - 1, middle), (0, middle - 1)]
    apart = [hop for hop in hops if set(hop) != {middle - 1, middle}]
    far = lax.ppermute(far, "member", apart + around if relayed(members) else hops)
    near = lax.ppermute(near, "member", hops)
    partner = lax.ppermute(own, "member", [(i, i ^ 1) for i in range(members)])
    if relayed(members):
        first, _ = lax.optimization_barrier((far, partner))
        return (own, partner, near, far, lax.ppermute(first, "member", onward))
    return (own, partner, near, far)


def body(doc_mantissa, doc_exponent, doc_home, block_cluster):
    rows, features = doc_mantissa.shape
    members = lax.axis_size("member")
    devices = lax.axis_size("group") * members
    capacity = rows // devices * 3 // 2
    member = lax.axis_index("member").reshape(1)
    sends = []
    guide = (doc_home[None, :], doc_exponent[None, :])
    for c, width in enumerate(CHUNKS):
        sent = pack(doc_mantissa, guide, sum(CHUNKS[:c]), width, devices, capacity)
        if c == 0:
            sent, guide = sent
        sends.append(sent)

    chunks = []
    order = score = None
    for c in range(len(CHUNKS)):
        got = lax.all_to_all(
            sends[c].reshape(devices, capacity, -1), ("group", "member"), 0, 0, tiled=True
        ).reshape(devices * capacity, -1)
        if c > 0:
            got, _ = lax.optimization_barrier((got, chunks[-1]))
        parts, order = unpack(got, order, rows)
        chunks.append(neighbours(*parts, members))
    for c, chunk in enumerate(chunks[:-1]):
        score = partial_scores(member, members, block_cluster, chunk, score)
        if c == 0:
            score, factor = score
    embed_sum, log_density = finish(
        member, members, block_cluster, chunks, score, factor, features
    )
    return embed_sum, log_density.reshape(rows)


def solution(mesh):
    return jax.shard_map(
        body,
        mesh=mesh,
        in_specs=(
            P(("group", "member"), None),
            P(("group", "member")),
            P(("group", "member")),
            P("group", None),
        ),
        out_specs=(P(("group", "member"), None), P(("group", "member"))),
        check_vma=False,
    )
```

```python
import jax
import jax.numpy as jnp
from jax import lax
from jax.experimental import pallas as pl
from jax.experimental.pallas import tpu as pltpu
from jax.sharding import PartitionSpec as P

BLK = 256
B_DEV = 2
SPAN = 2
RUN = SPAN + 1
WINDOW = B_DEV + 2 * SPAN
META = 128
KERNEL_SHIFT = 4.0
EPSILON = 1e-06
CHUNKS = (2048, 2048)
PIECE = 512

F32 = jnp.float32
BF16 = jnp.bfloat16
VM = pl.BlockSpec(memory_space=pltpu.VMEM)
SM = pl.BlockSpec(memory_space=pltpu.SMEM)
HBM = pl.BlockSpec(memory_space=pltpu.HBM)
WHOLE = pltpu.CompilerParams(vmem_limit_bytes=64 * 1024 * 1024)


def halfway(width):
    return (width // 2) // BLK * BLK


def steps(width):
    cut = halfway(width)
    return [
        (at, min(PIECE, end - at))
        for begin, end in ((0, cut), (cut, width))
        for at in range(begin, end, PIECE)
    ]


def relayed(members):
    return members == 8


def column_of(row):
    return jnp.broadcast_to(row, (128, row.shape[1])).T[:, 0:1]


def row_of(column):
    return jnp.broadcast_to(column, (column.shape[0], 128)).T[0:1]


def pack(doc, guide, offset, width, devices, capacity):
    rows, features = doc.shape
    slots = devices * capacity
    first = isinstance(guide, tuple)
    tail = META if first else 0
    pieces = steps(width)
    rest = [(at, min(PIECE, features - at)) for at in range(width, features, PIECE)] if first else []
    count = len(pieces)

    def kernel(*refs):
        if first:
            home_ref, exponent_ref, doc_ref, out_ref, order_ref, tile, packed, sems = refs
        else:
            order_ref, doc_ref, out_ref, tile, packed, sems = refs
        loads, stores = [], []
        for p, (at, wide) in enumerate(pieces + rest):
            loads.append(
                pltpu.make_async_copy(
                    doc_ref.at[:, pl.ds(offset + at, wide)], tile.at[:, pl.ds(at, wide)], sems.at[p]
                )
            )
            loads[-1].start()

        def send(begin, end):
            piece = pl.ds(begin, end - begin)
            stores.append(
                pltpu.make_async_copy(
                    packed.at[:, piece], out_ref.at[:, piece], sems.at[len(loads) + len(stores)]
                )
            )
            stores[-1].start()

        if first:
            home = home_ref[...].astype(F32)
            target = jnp.floor((home + 0.5) * (1.0 / rows))
            target_col = column_of(target)
            earlier = lax.broadcasted_iota(jnp.int32, (rows, rows), 0) < lax.broadcasted_iota(
                jnp.int32, (rows, rows), 1
            )
            rank = jnp.sum(
                jnp.where(earlier & (target_col == target), 1.0, 0.0), axis=0, keepdims=True
            )
            position = (target * capacity + rank).astype(jnp.int32)
            order = jnp.where(
                lax.broadcasted_iota(jnp.int32, (slots, rows), 0) == position, 1.0, 0.0
            ).astype(BF16)
            order_ref[...] = order
        else:
            order = order_ref[...]
        for p, (at, wide) in enumerate(pieces):
            loads[p].wait()
            packed[:, at : at + wide] = jnp.dot(
                order, tile[:, at : at + wide], preferred_element_type=F32
            ).astype(BF16)
            send(at, at + wide)
        if first:
            for load in loads[count:]:
                load.wait()
            total = jnp.zeros((rows, 128), F32)
            for at in range(0, features, 128):
                values = tile[:, at : at + 128].astype(F32)
                total = total + values * values
            square = row_of(jnp.sum(total, axis=1, keepdims=True))
            inverse = lax.rsqrt(square * (1.0 / features) + EPSILON)
            high = inverse.astype(BF16).astype(F32)
            middle = (inverse - high).astype(BF16).astype(F32)
            slot = home - target * rows
            slot_high = jnp.floor((slot + 0.5) * (1.0 / 32))
            field = lax.broadcasted_iota(jnp.int32, (META, rows), 0)
            meta = jnp.where(field == 0, 1.0, 0.0)
            for f, value in enumerate(
                (
                    slot_high,
                    slot - slot_high * 32,
                    exponent_ref[...].astype(F32),
                    high,
                    middle,
                    inverse - high - middle,
                ),
                1,
            ):
                meta = jnp.where(field == f, value, meta)
            packed[:, width:] = lax.dot_general(
                order, meta.astype(BF16), (((1,), (1,)), ((), ())), preferred_element_type=F32
            ).astype(BF16)
            send(width, width + META)
        for copy in stores:
            copy.wait()

    sent = jax.ShapeDtypeStruct((slots, width + tail), BF16)
    return pl.pallas_call(
        kernel,
        in_specs=[VM, VM, HBM] if first else [VM, HBM],
        out_specs=(HBM, VM) if first else HBM,
        out_shape=(sent, jax.ShapeDtypeStruct((slots, rows), BF16)) if first else sent,
        scratch_shapes=[
            pltpu.VMEM((rows, features if first else width), BF16),
            pltpu.VMEM((slots, width + tail), BF16),
            pltpu.SemaphoreType.DMA((2 * count + len(rest) + 1,)),
        ],
        compiler_params=WHOLE,
        name="pack_first" if first else "pack_next",
    )(*(guide if first else (guide,)), doc)


def unpack(got, order, rows):
    slots, width = got.shape
    first = order is None
    pieces = steps(width)
    count = len(pieces)
    cut = halfway(width)

    def kernel(*refs):
        got_ref = refs[0]
        outs = 1 if first else 2
        out_refs = refs[outs : outs + 3]
        if first:
            order_ref, tile, placed, sems = refs[outs + 3 :]
        else:
            order_ref = refs[1]
            tile, placed, sems = refs[outs + 3 :]
        loads, stores = [], []
        for p in ([count - 1] if first else []) + list(range(count - 1 if first else count)):
            at, wide = pieces[p]
            piece = pl.ds(at, wide)
            loads.append((p, pltpu.make_async_copy(got_ref.at[:, piece], tile.at[:, piece], sems.at[p])))
            loads[-1][1].start()
        if first:
            loads[0][1].wait()
            fields = tile[:, width - META :].astype(F32)
            slot = fields[:, 1:2] * 32 + fields[:, 2:3]
            home = lax.broadcasted_iota(jnp.int32, (slots, rows), 1).astype(F32)
            hit = (home == slot) & (fields[:, 0:1] > 0.5)
            order = jnp.where(hit, 1.0, 0.0).T.astype(BF16)
            order_ref[...] = order
        else:
            order = order_ref[...]
        for number, (p, load) in enumerate(loads):
            at, wide = pieces[p]
            if number > 0 or not first:
                load.wait()
            placed[:, at : at + wide] = jnp.dot(
                order, tile[:, at : at + wide], preferred_element_type=F32
            ).astype(BF16)
            source = placed.at[:, pl.ds(at, wide)]
            half, inner = (1, at) if at < cut else (2, at - cut)
            for target in (
                out_refs[half].at[:, pl.ds(inner, wide)],
                out_refs[0].at[:, pl.ds(at, wide)],
            ):
                stores.append(pltpu.make_async_copy(source, target, sems.at[count + len(stores)]))
                stores[-1].start()
        for copy in stores:
            copy.wait()

    outs = [jax.ShapeDtypeStruct((rows, columns), BF16) for columns in (width, cut, width - cut)]
    if first:
        outs.append(jax.ShapeDtypeStruct((rows, slots), BF16))
    result = pl.pallas_call(
        kernel,
        in_specs=[HBM] if first else [HBM, VM],
        out_specs=[HBM] * 3 + [VM] * first,
        out_shape=outs,
        scratch_shapes=[
            pltpu.VMEM(got.shape, BF16),
            pltpu.VMEM((rows, width), BF16),
            pltpu.SemaphoreType.DMA((3 * count,)),
        ],
        compiler_params=WHOLE if first else None,
        name="unpack_first" if first else "unpack_next",
    )(*((got,) if first else (got, order)))
    return result[:3], result[3] if first else order


def runs(member_ref, cluster_ref):
    blocks = cluster_ref.shape[1]
    base = member_ref[0] * B_DEV

    def cluster(index):
        inside = (index >= 0) & (index < blocks)
        return jnp.where(inside, cluster_ref[0, jnp.clip(index, 0, blocks - 1)], -1)

    result = []
    for b in range(B_DEV):
        mine = cluster(base + b)
        back = jnp.where(
            cluster(base + b - 2) == mine, 2, jnp.where(cluster(base + b - 1) == mine, 1, 0)
        )
        links = [
            jnp.where(cluster(base + b - back + k) == mine, 1, 0) for k in range(RUN)
        ]
        result.append((back, links))
    return result


def load_window(member_ref, members, parts, window, sems, column):
    own, partner, near, far = parts[:4]
    rows, width = own.shape
    cut = halfway(width)
    member = member_ref[0]
    partner_at = pl.multiple_of((1 - member % 2) * 2 * rows, rows)
    other_at = pl.multiple_of((member % 2) * 2 * rows, rows)
    middle = (member == members // 2) | (member == members // 2 - 1)
    groups = []
    for at, wide in steps(width):
        piece = pl.ds(at, wide)
        target = pl.ds(column + at, wide)
        half, inner = (near, at) if at < cut else (far, at - cut)
        group = [
            pltpu.make_async_copy(source, window.at[pl.ds(begin, rows), target], sems.at[len(groups), n])
            for n, (source, begin) in enumerate(
                (
                    (own.at[:, piece], rows),
                    (partner.at[:, piece], partner_at),
                    (half.at[:, pl.ds(inner, wide)], other_at),
                )
            )
        ]
        group[0].start()
        group[1].start()
        if at < cut or len(parts) == 4:
            group[2].start()
        else:
            relay = pltpu.make_async_copy(
                parts[4].at[:, pl.ds(inner, wide)],
                window.at[pl.ds(other_at, rows), target],
                sems.at[len(groups), 2],
            )
            pl.when(middle)(relay.start)
            pl.when(jnp.logical_not(middle))(group[2].start)
        groups.append((column + at, wide, group))
    return groups


def run_scores(window, back, b, column, width):
    first = pl.multiple_of((SPAN + b - back) * BLK, BLK)
    return lax.dot_general(
        window[(SPAN + b) * BLK : (SPAN + b + 1) * BLK, column : column + width],
        window[pl.ds(first, RUN * BLK), column : column + width],
        (((1,), (1,)), ((), ())),
        preferred_element_type=F32,
    )


def partial_scores(member, members, cluster, parts, score):
    rows, width = parts[0].shape
    given = score is not None
    number = len(parts)

    def kernel(member_ref, cluster_ref, *refs):
        if given:
            score_in, score_ref, window, sems = refs[number:]
        else:
            score_ref, factor_ref, window, sems = refs[number:]
        found = runs(member_ref, cluster_ref)
        groups = load_window(member_ref, members, refs[:number], window, sems, 0)
        for p, (column, wide, group) in enumerate(groups):
            for copy in group:
                copy.wait()
            if not given:
                wide = min(wide, width - META - column)
            if wide == 0:
                continue
            for b in range(B_DEV):
                value = run_scores(window, found[b][0], b, column, wide)
                if p > 0:
                    value = value + score_ref[b]
                elif given:
                    value = value + score_in[b]
                score_ref[b] = value
        if not given:
            for side in range(3):
                fields = window[side * rows : (side + 1) * rows, width - META :].astype(F32).T
                field = lax.broadcasted_iota(jnp.int32, (8, rows), 0)
                inverse = fields[4:5] + fields[5:6] + fields[6:7]
                factor_ref[side] = jnp.where(field == 0, inverse, jnp.exp2(fields[3:4]))

    score_shape = jax.ShapeDtypeStruct((B_DEV, BLK, RUN * BLK), F32)
    return pl.pallas_call(
        kernel,
        in_specs=[SM, SM] + [HBM] * number + [VM] * given,
        out_shape=score_shape if given else (score_shape, jax.ShapeDtypeStruct((3, 8, rows), F32)),
        scratch_shapes=[
            pltpu.VMEM((3 * rows, width), BF16),
            pltpu.SemaphoreType.DMA((len(steps(width)), 3)),
        ],
        compiler_params=WHOLE,
        name="partial_scores",
    )(member, cluster, *parts, *([score] if given else []))


def finish(member, members, cluster, chunks, score, factor, features):
    rows = chunks[0][0].shape[0]
    count = len(chunks)
    widths = [chunk[0].shape[1] for chunk in chunks]
    pieces = [len(steps(width)) for width in widths]
    number = len(chunks[0])
    last = count - 1

    def kernel(member_ref, cluster_ref, *refs):
        parts = [refs[number * c : number * (c + 1)] for c in range(count)]
        score_in, factor_in, out_ref, log_ref = refs[number * count : number * count + 4]
        window, packed, value_ref, factor_ref, early_sems, out_sems = refs[
            number * count + 4 : number * count + 10
        ]
        load_sems = refs[number * count + 10 :]
        found = runs(member_ref, cluster_ref)
        loads = {}

        def load(c):
            loads[c] = load_window(
                member_ref, members, parts[c], window, load_sems[c], sum(widths[:c])
            )

        load(last)
        early = [
            pltpu.make_async_copy(score_in, value_ref, early_sems.at[0]),
            pltpu.make_async_copy(factor_in, factor_ref, early_sems.at[1]),
        ]
        for copy in early:
            copy.start()
        for c in range(last):
            load(c)
        for copy in early:
            copy.wait()
        for column, wide, group in loads[last]:
            for copy in group:
                copy.wait()
            for b in range(B_DEV):
                value_ref[b] += run_scores(window, found[b][0], b, column, wide)
        apart = lax.broadcasted_iota(jnp.int32, (BLK, BLK), 0) - lax.broadcasted_iota(
            jnp.int32, (BLK, BLK), 1
        )
        weights = []
        for b in range(B_DEV):
            back, links = found[b]
            mine = factor_ref[1, :, b * BLK : (b + 1) * BLK]
            row_scale = column_of(mine[0:1]) * features**-0.5
            density = jnp.zeros((BLK, 1), F32)
            tiles = []
            for k in range(RUN):
                block = SPAN + b - back + k
                far = factor_ref[block // B_DEV, :, pl.ds(pl.multiple_of((block % B_DEV) * BLK, BLK), BLK)]
                value = jnp.exp(
                    value_ref[b, :, k * BLK : (k + 1) * BLK] * row_scale * far[0:1] - KERNEL_SHIFT
                )
                kept = (apart + jnp.where(back == k, 0, 2 * BLK) != 0) & (
                    jnp.full((BLK, BLK), links[k], jnp.int32) > 0
                )
                value = jnp.where(kept, value, 0.0)
                density = density + jnp.sum(value, axis=1, keepdims=True)
                tiles.append((value.astype(BF16).astype(F32) * far[1:2]).astype(BF16))
            weights.append(jnp.concatenate(tiles, axis=1))
            log_ref[:, b * BLK : (b + 1) * BLK] = jnp.log(row_of(density))
        outgoing = []
        for c in [last] + list(range(last)):
            for column, wide, group in loads[c]:
                if c != last:
                    for copy in group:
                        copy.wait()
                if c == 0:
                    wide = min(wide, widths[0] - META - column)
                    if wide == 0:
                        continue
                out_at = column if c == 0 else column - META
                for b in range(B_DEV):
                    first = pl.multiple_of((SPAN + b - found[b][0]) * BLK, BLK)
                    packed[b * BLK : (b + 1) * BLK, out_at : out_at + wide] = jnp.dot(
                        weights[b],
                        window[pl.ds(first, RUN * BLK), column : column + wide],
                        preferred_element_type=F32,
                    ).astype(BF16)
                piece = pl.ds(out_at, wide)
                copy = pltpu.make_async_copy(
                    packed.at[:, piece], out_ref.at[:, piece], out_sems.at[len(outgoing)]
                )
                copy.start()
                outgoing.append(copy)
        for copy in outgoing:
            copy.wait()

    flat = [ref for chunk in chunks for ref in chunk]
    return pl.pallas_call(
        kernel,
        in_specs=[SM, SM] + [HBM] * (len(flat) + 2),
        out_specs=(HBM, VM),
        out_shape=(
            jax.ShapeDtypeStruct((rows, features), BF16),
            jax.ShapeDtypeStruct((1, rows), F32),
        ),
        scratch_shapes=[
            pltpu.VMEM((3 * rows, features + META), BF16),
            pltpu.VMEM((rows, features), BF16),
            pltpu.VMEM((B_DEV, BLK, RUN * BLK), F32),
            pltpu.VMEM((3, 8, rows), F32),
            pltpu.SemaphoreType.DMA((2,)),
            pltpu.SemaphoreType.DMA((sum(pieces),)),
        ]
        + [pltpu.SemaphoreType.DMA((pieces_of, 3)) for pieces_of in pieces],
        compiler_params=WHOLE,
        name="finish",
    )(member, cluster, *flat, score, factor)


def neighbours(own, near, far, members, beside):
    middle = members // 2
    odd = range(1, members - 1, 2)
    hops = [(i, i + 1) for i in odd] + [(i + 1, i) for i in odd]
    around = [(middle - 1, members - 1), (middle, 0)]
    onward = [(members - 1, middle), (0, middle - 1)]
    apart = [hop for hop in hops if set(hop) != {middle - 1, middle}]
    far = lax.ppermute(far, "member", apart + around if relayed(members) else hops)
    near = lax.ppermute(near, "member", hops)
    partner = lax.ppermute(own, "member", [(i, i ^ 1) for i in range(members)])
    if relayed(members):
        first = far
        if beside:
            first, _ = lax.optimization_barrier((far, partner))
        return (own, partner, near, far, lax.ppermute(first, "member", onward))
    return (own, partner, near, far)


def body(doc_mantissa, doc_exponent, doc_home, block_cluster):
    rows, features = doc_mantissa.shape
    members = lax.axis_size("member")
    devices = lax.axis_size("group") * members
    capacity = rows // devices * 3 // 2
    member = lax.axis_index("member").reshape(1)
    sends = []
    guide = (doc_home[None, :], doc_exponent[None, :])
    for c, width in enumerate(CHUNKS):
        sent = pack(doc_mantissa, guide, sum(CHUNKS[:c]), width, devices, capacity)
        if c == 0:
            sent, guide = sent
        sends.append(sent)

    chunks = []
    order = score = None
    for c in range(len(CHUNKS)):
        got = lax.all_to_all(
            sends[c].reshape(devices, capacity, -1), ("group", "member"), 0, 0, tiled=True
        ).reshape(devices * capacity, -1)
        if c > 0:
            got, _ = lax.optimization_barrier((got, chunks[-1]))
        parts, order = unpack(got, order, rows)
        chunks.append(neighbours(*parts, members, c + 1 < len(CHUNKS)))
    for c, chunk in enumerate(chunks[:-1]):
        score = partial_scores(member, members, block_cluster, chunk, score)
        if c == 0:
            score, factor = score
    embed_sum, log_density = finish(
        member, members, block_cluster, chunks, score, factor, features
    )
    return embed_sum, log_density.reshape(rows)


def solution(mesh):
    return jax.shard_map(
        body,
        mesh=mesh,
        in_specs=(
            P(("group", "member"), None),
            P(("group", "member")),
            P(("group", "member")),
            P("group", None),
        ),
        out_specs=(P(("group", "member"), None), P(("group", "member"))),
        check_vma=False,
    )
```

```python
import jax
import jax.numpy as jnp
from jax import lax
from jax.experimental import pallas as pl
from jax.experimental.pallas import tpu as pltpu
from jax.sharding import PartitionSpec as P

BLK = 256
B_DEV = 2
SPAN = 2
RUN = SPAN + 1
WINDOW = B_DEV + 2 * SPAN
META = 128
KERNEL_SHIFT = 4.0
EPSILON = 1e-06
CHUNKS = (1536, 1408, 1152)
PIECE = 768

F32 = jnp.float32
BF16 = jnp.bfloat16
VM = pl.BlockSpec(memory_space=pltpu.VMEM)
SM = pl.BlockSpec(memory_space=pltpu.SMEM)
HBM = pl.BlockSpec(memory_space=pltpu.HBM)
WHOLE = pltpu.CompilerParams(vmem_limit_bytes=64 * 1024 * 1024)


def halfway(width):
    return (width // 2) // 128 * 128


def steps(width):
    cut = halfway(width)
    return [
        (at, min(PIECE, end - at))
        for begin, end in ((0, cut), (cut, width))
        for at in range(begin, end, PIECE)
    ]


def relayed(members):
    return members == 8


def column_of(row):
    return jnp.broadcast_to(row, (128, row.shape[1])).T[:, 0:1]


def row_of(column):
    return jnp.broadcast_to(column, (column.shape[0], 128)).T[0:1]


def pack(doc, guide, offset, width, devices, capacity):
    rows, features = doc.shape
    slots = devices * capacity
    first = isinstance(guide, tuple)
    tail = META if first else 0
    pieces = steps(width)
    rest = [(at, min(PIECE, features - at)) for at in range(width, features, PIECE)] if first else []
    count = len(pieces)

    def kernel(*refs):
        if first:
            home_ref, exponent_ref, doc_ref, out_ref, order_ref, tile, packed, sems = refs
        else:
            order_ref, doc_ref, out_ref, tile, packed, sems = refs
        loads, stores = [], []
        for p, (at, wide) in enumerate(pieces + rest):
            loads.append(
                pltpu.make_async_copy(
                    doc_ref.at[:, pl.ds(offset + at, wide)], tile.at[:, pl.ds(at, wide)], sems.at[p]
                )
            )
            loads[-1].start()

        def send(begin, end):
            piece = pl.ds(begin, end - begin)
            stores.append(
                pltpu.make_async_copy(
                    packed.at[:, piece], out_ref.at[:, piece], sems.at[len(loads) + len(stores)]
                )
            )
            stores[-1].start()

        if first:
            home = home_ref[...].astype(F32)
            target = jnp.floor((home + 0.5) * (1.0 / rows))
            target_col = column_of(target)
            earlier = lax.broadcasted_iota(jnp.int32, (rows, rows), 0) < lax.broadcasted_iota(
                jnp.int32, (rows, rows), 1
            )
            rank = jnp.sum(
                jnp.where(earlier & (target_col == target), 1.0, 0.0), axis=0, keepdims=True
            )
            position = (target * capacity + rank).astype(jnp.int32)
            order = jnp.where(
                lax.broadcasted_iota(jnp.int32, (slots, rows), 0) == position, 1.0, 0.0
            ).astype(BF16)
            order_ref[...] = order
        else:
            order = order_ref[...]
        for p, (at, wide) in enumerate(pieces):
            loads[p].wait()
            packed[:, at : at + wide] = jnp.dot(
                order, tile[:, at : at + wide], preferred_element_type=F32
            ).astype(BF16)
            send(at, at + wide)
        if first:
            for load in loads[count:]:
                load.wait()
            total = jnp.zeros((rows, 128), F32)
            for at in range(0, features, 128):
                values = tile[:, at : at + 128].astype(F32)
                total = total + values * values
            square = row_of(jnp.sum(total, axis=1, keepdims=True))
            inverse = lax.rsqrt(square * (1.0 / features) + EPSILON)
            high = inverse.astype(BF16).astype(F32)
            middle = (inverse - high).astype(BF16).astype(F32)
            slot = home - target * rows
            slot_high = jnp.floor((slot + 0.5) * (1.0 / 32))
            field = lax.broadcasted_iota(jnp.int32, (META, rows), 0)
            meta = jnp.where(field == 0, 1.0, 0.0)
            for f, value in enumerate(
                (
                    slot_high,
                    slot - slot_high * 32,
                    exponent_ref[...].astype(F32),
                    high,
                    middle,
                    inverse - high - middle,
                ),
                1,
            ):
                meta = jnp.where(field == f, value, meta)
            packed[:, width:] = lax.dot_general(
                order, meta.astype(BF16), (((1,), (1,)), ((), ())), preferred_element_type=F32
            ).astype(BF16)
            send(width, width + META)
        for copy in stores:
            copy.wait()

    sent = jax.ShapeDtypeStruct((slots, width + tail), BF16)
    return pl.pallas_call(
        kernel,
        in_specs=[VM, VM, HBM] if first else [VM, HBM],
        out_specs=(HBM, VM) if first else HBM,
        out_shape=(sent, jax.ShapeDtypeStruct((slots, rows), BF16)) if first else sent,
        scratch_shapes=[
            pltpu.VMEM((rows, features if first else width), BF16),
            pltpu.VMEM((slots, width + tail), BF16),
            pltpu.SemaphoreType.DMA((2 * count + len(rest) + 1,)),
        ],
        compiler_params=WHOLE,
        name="pack_first" if first else "pack_next",
    )(*(guide if first else (guide,)), doc)


def unpack(got, order, rows):
    slots, width = got.shape
    first = order is None
    cut = halfway(width)

    def kernel(*refs):
        if first:
            got_ref, own_ref, near_ref, far_ref, order_ref, tile, placed, sems = refs
        else:
            got_ref, order_in, own_ref, near_ref, far_ref, tile, placed, order_ref, sems = refs
            given = pltpu.make_async_copy(order_in, order_ref, sems.at[0])
            given.start()
        begins = [width - META, 0] if first else [0]
        loads = []
        for n, begin in enumerate(begins):
            piece = pl.ds(begin, META if first and n == 0 else width - META * first)
            loads.append(
                pltpu.make_async_copy(got_ref.at[:, piece], tile.at[:, piece], sems.at[1 + n])
            )
            loads[-1].start()
        loads[0].wait()
        if first:
            fields = tile[:, width - META :].astype(F32)
            slot = fields[:, 1:2] * 32 + fields[:, 2:3]
            home = lax.broadcasted_iota(jnp.int32, (slots, rows), 1).astype(F32)
            hit = (home == slot) & (fields[:, 0:1] > 0.5)
            order_ref[...] = jnp.where(hit, 1.0, 0.0).T.astype(BF16)
            loads[1].wait()
        else:
            given.wait()
        stores = []
        for n, (begin, end, ref) in enumerate(((cut, width, far_ref), (0, cut, near_ref))):
            placed[:, begin:end] = jnp.dot(
                order_ref[...], tile[:, begin:end], preferred_element_type=F32
            ).astype(BF16)
            piece = pl.ds(begin, end - begin)
            for m, target in enumerate((ref, own_ref.at[:, piece])):
                stores.append(
                    pltpu.make_async_copy(placed.at[:, piece], target, sems.at[3 + 2 * n + m])
                )
                stores[-1].start()
        for copy in stores:
            copy.wait()

    outs = [jax.ShapeDtypeStruct((rows, columns), BF16) for columns in (width, cut, width - cut)]
    if first:
        outs.append(jax.ShapeDtypeStruct((rows, slots), BF16))
    result = pl.pallas_call(
        kernel,
        in_specs=[HBM] if first else [HBM, HBM],
        out_specs=[HBM] * 3 + [VM] * first,
        out_shape=outs,
        scratch_shapes=[pltpu.VMEM(got.shape, BF16), pltpu.VMEM((rows, width), BF16)]
        + [pltpu.VMEM((rows, slots), BF16)] * (not first)
        + [pltpu.SemaphoreType.DMA((7,))],
        compiler_params=WHOLE,
        name="unpack_first" if first else "unpack_next",
    )(*((got,) if first else (got, order)))
    return result[:3], result[3] if first else order


def runs(member_ref, cluster_ref):
    blocks = cluster_ref.shape[1]
    base = member_ref[0] * B_DEV

    def cluster(index):
        inside = (index >= 0) & (index < blocks)
        return jnp.where(inside, cluster_ref[0, jnp.clip(index, 0, blocks - 1)], -1)

    result = []
    for b in range(B_DEV):
        mine = cluster(base + b)
        back = jnp.where(
            cluster(base + b - 2) == mine, 2, jnp.where(cluster(base + b - 1) == mine, 1, 0)
        )
        links = [
            jnp.where(cluster(base + b - back + k) == mine, 1, 0) for k in range(RUN)
        ]
        result.append((back, links))
    return result


def load_window(member_ref, members, parts, window, sems):
    own, partner, near, far = parts[:4]
    rows, width = own.shape
    cut = halfway(width)
    member = member_ref[0]
    partner_at = pl.multiple_of((1 - member % 2) * 2 * rows, rows)
    other_at = pl.multiple_of((member % 2) * 2 * rows, rows)
    middle = (member == members // 2) | (member == members // 2 - 1)
    second = window.at[pl.ds(other_at, rows), pl.ds(cut, width - cut)]
    copies = [
        pltpu.make_async_copy(source, target, sems.at[n])
        for n, (source, target) in enumerate(
            (
                (own, window.at[pl.ds(rows, rows)]),
                (partner, window.at[pl.ds(partner_at, rows)]),
                (near, window.at[pl.ds(other_at, rows), pl.ds(0, cut)]),
                (far, second),
            )
        )
    ]
    for copy in copies[:3]:
        copy.start()
    if len(parts) == 4:
        copies[3].start()
    else:
        relay = pltpu.make_async_copy(parts[4], second, sems.at[3])
        pl.when(middle)(relay.start)
        pl.when(jnp.logical_not(middle))(copies[3].start)
    return copies


def run_scores(window, back, b, width):
    first = pl.multiple_of((SPAN + b - back) * BLK, BLK)
    return lax.dot_general(
        window[(SPAN + b) * BLK : (SPAN + b + 1) * BLK, 0:width],
        window[pl.ds(first, RUN * BLK), 0:width],
        (((1,), (1,)), ((), ())),
        preferred_element_type=F32,
    )


def partial_scores(member, members, cluster, parts, score):
    rows, width = parts[0].shape
    given = score is not None
    number = len(parts)

    def kernel(member_ref, cluster_ref, *refs):
        if given:
            score_in, score_ref, window, sems = refs[number:]
        else:
            score_ref, factor_ref, window, sems = refs[number:]
        found = runs(member_ref, cluster_ref)
        for copy in load_window(member_ref, members, refs[:number], window, sems):
            copy.wait()
        for b in range(B_DEV):
            value = run_scores(window, found[b][0], b, width if given else width - META)
            score_ref[b] = value + score_in[b] if given else value
        if not given:
            for side in range(3):
                fields = window[side * rows : (side + 1) * rows, width - META :].astype(F32).T
                field = lax.broadcasted_iota(jnp.int32, (8, rows), 0)
                inverse = fields[4:5] + fields[5:6] + fields[6:7]
                factor_ref[side] = jnp.where(field == 0, inverse, jnp.exp2(fields[3:4]))

    score_shape = jax.ShapeDtypeStruct((B_DEV, BLK, RUN * BLK), F32)
    return pl.pallas_call(
        kernel,
        in_specs=[SM, SM] + [HBM] * number + [VM] * given,
        out_shape=score_shape if given else (score_shape, jax.ShapeDtypeStruct((3, 8, rows), F32)),
        scratch_shapes=[
            pltpu.VMEM((3 * rows, width), BF16),
            pltpu.SemaphoreType.DMA((4,)),
        ],
        compiler_params=WHOLE,
        name="partial_scores",
    )(member, cluster, *parts, *([score] if given else []))


def finish(member, members, cluster, chunks, score, factor, features):
    rows = chunks[0][0].shape[0]
    count = len(chunks)
    widths = [chunk[0].shape[1] for chunk in chunks]
    number = len(chunks[0])
    last = count - 1

    def kernel(member_ref, cluster_ref, *refs):
        parts = [refs[number * c : number * (c + 1)] for c in range(count)]
        score_in, factor_in, out_ref, log_ref = refs[number * count : number * count + 4]
        packed, value_ref, factor_ref, early_sems, out_sems, load_sems = refs[
            number * count + 4 : number * count + 10
        ]
        windows = refs[number * count + 10 :]
        found = runs(member_ref, cluster_ref)
        loads = {}

        def load(c):
            loads[c] = load_window(member_ref, members, parts[c], windows[c], load_sems.at[c])

        load(last)
        early = [
            pltpu.make_async_copy(score_in, value_ref, early_sems.at[0]),
            pltpu.make_async_copy(factor_in, factor_ref, early_sems.at[1]),
        ]
        for copy in early:
            copy.start()
        for c in range(last):
            load(c)
        for copy in early:
            copy.wait()
        for copy in loads[last]:
            copy.wait()
        for b in range(B_DEV):
            value_ref[b] += run_scores(windows[last], found[b][0], b, widths[last])
        apart = lax.broadcasted_iota(jnp.int32, (BLK, BLK), 0) - lax.broadcasted_iota(
            jnp.int32, (BLK, BLK), 1
        )
        weights = []
        for b in range(B_DEV):
            back, links = found[b]
            mine = factor_ref[1, :, b * BLK : (b + 1) * BLK]
            row_scale = column_of(mine[0:1]) * features**-0.5
            density = jnp.zeros((BLK, 1), F32)
            tiles = []
            for k in range(RUN):
                block = SPAN + b - back + k
                far = factor_ref[block // B_DEV, :, pl.ds(pl.multiple_of((block % B_DEV) * BLK, BLK), BLK)]
                value = jnp.exp(
                    value_ref[b, :, k * BLK : (k + 1) * BLK] * row_scale * far[0:1] - KERNEL_SHIFT
                )
                kept = (apart + jnp.where(back == k, 0, 2 * BLK) != 0) & (
                    jnp.full((BLK, BLK), links[k], jnp.int32) > 0
                )
                value = jnp.where(kept, value, 0.0)
                density = density + jnp.sum(value, axis=1, keepdims=True)
                tiles.append((value.astype(BF16).astype(F32) * far[1:2]).astype(BF16))
            weights.append(jnp.concatenate(tiles, axis=1))
            log_ref[:, b * BLK : (b + 1) * BLK] = jnp.log(row_of(density))
        outgoing = []
        for c in [last] + list(range(last)):
            if c != last:
                for copy in loads[c]:
                    copy.wait()
            out_at = sum(CHUNKS[:c])
            for at, wide in steps(CHUNKS[c]):
                for b in range(B_DEV):
                    first = pl.multiple_of((SPAN + b - found[b][0]) * BLK, BLK)
                    packed[b * BLK : (b + 1) * BLK, out_at + at : out_at + at + wide] = jnp.dot(
                        weights[b],
                        windows[c][pl.ds(first, RUN * BLK), at : at + wide],
                        preferred_element_type=F32,
                    ).astype(BF16)
                piece = pl.ds(out_at + at, wide)
                copy = pltpu.make_async_copy(
                    packed.at[:, piece], out_ref.at[:, piece], out_sems.at[len(outgoing)]
                )
                copy.start()
                outgoing.append(copy)
        for copy in outgoing:
            copy.wait()

    flat = [ref for chunk in chunks for ref in chunk]
    return pl.pallas_call(
        kernel,
        in_specs=[SM, SM] + [HBM] * (len(flat) + 2),
        out_specs=(HBM, VM),
        out_shape=(
            jax.ShapeDtypeStruct((rows, features), BF16),
            jax.ShapeDtypeStruct((1, rows), F32),
        ),
        scratch_shapes=[
            pltpu.VMEM((rows, features), BF16),
            pltpu.VMEM((B_DEV, BLK, RUN * BLK), F32),
            pltpu.VMEM((3, 8, rows), F32),
            pltpu.SemaphoreType.DMA((2,)),
            pltpu.SemaphoreType.DMA((sum(len(steps(width)) for width in CHUNKS),)),
            pltpu.SemaphoreType.DMA((count, 4)),
        ]
        + [pltpu.VMEM((3 * rows, width), BF16) for width in widths],
        compiler_params=WHOLE,
        name="finish",
    )(member, cluster, *flat, score, factor)


def neighbours(own, near, far, members, beside):
    middle = members // 2
    odd = range(1, members - 1, 2)
    hops = [(i, i + 1) for i in odd] + [(i + 1, i) for i in odd]
    around = [(middle - 1, members - 1), (middle, 0)]
    onward = [(members - 1, middle), (0, middle - 1)]
    apart = [hop for hop in hops if set(hop) != {middle - 1, middle}]
    far = lax.ppermute(far, "member", apart + around if relayed(members) else hops)
    near = lax.ppermute(near, "member", hops)
    partner = lax.ppermute(own, "member", [(i, i ^ 1) for i in range(members)])
    if relayed(members):
        first = far
        if beside:
            first, _ = lax.optimization_barrier((far, partner))
        return (own, partner, near, far, lax.ppermute(first, "member", onward))
    return (own, partner, near, far)


def body(doc_mantissa, doc_exponent, doc_home, block_cluster):
    rows, features = doc_mantissa.shape
    members = lax.axis_size("member")
    devices = lax.axis_size("group") * members
    capacity = rows // devices * 3 // 2
    member = lax.axis_index("member").reshape(1)
    sends = []
    guide = (doc_home[None, :], doc_exponent[None, :])
    for c, width in enumerate(CHUNKS):
        sent = pack(doc_mantissa, guide, sum(CHUNKS[:c]), width, devices, capacity)
        if c == 0:
            sent, guide = sent
        sends.append(sent)

    chunks = []
    order = score = None
    for c in range(len(CHUNKS)):
        if c > 1:
            sends[c], _ = lax.optimization_barrier((sends[c], chunks[c - 2]))
        got = lax.all_to_all(
            sends[c].reshape(devices, capacity, -1), ("group", "member"), 0, 0, tiled=True
        ).reshape(devices * capacity, -1)
        if c > 0:
            got, _ = lax.optimization_barrier((got, chunks[-1]))
        parts, order = unpack(got, order, rows)
        chunks.append(neighbours(*parts, members, c + 1 < len(CHUNKS)))
    for c, chunk in enumerate(chunks[:-1]):
        score = partial_scores(member, members, block_cluster, chunk, score)
        if c == 0:
            score, factor = score
    embed_sum, log_density = finish(
        member, members, block_cluster, chunks, score, factor, features
    )
    return embed_sum, log_density.reshape(rows)


def solution(mesh):
    return jax.shard_map(
        body,
        mesh=mesh,
        in_specs=(
            P(("group", "member"), None),
            P(("group", "member")),
            P(("group", "member")),
            P("group", None),
        ),
        out_specs=(P(("group", "member"), None), P(("group", "member"))),
        check_vma=False,
    )
```

```python
import jax
import jax.numpy as jnp
from jax import lax
from jax.experimental import pallas as pl
from jax.experimental.pallas import tpu as pltpu
from jax.sharding import PartitionSpec as P

BLK = 256
B_DEV = 2
SPAN = 2
RUN = SPAN + 1
WINDOW = B_DEV + 2 * SPAN
META = 128
KERNEL_SHIFT = 4.0
EPSILON = 1e-06
CHUNKS = (1536, 1408, 1152)
PIECE = 768

F32 = jnp.float32
BF16 = jnp.bfloat16
VM = pl.BlockSpec(memory_space=pltpu.VMEM)
SM = pl.BlockSpec(memory_space=pltpu.SMEM)
HBM = pl.BlockSpec(memory_space=pltpu.HBM)
WHOLE = pltpu.CompilerParams(vmem_limit_bytes=64 * 1024 * 1024)


def halfway(width):
    return -(-width // 256) * 128


def steps(width):
    cut = halfway(width)
    return [
        (at, min(PIECE, end - at))
        for begin, end in ((0, cut), (cut, width))
        for at in range(begin, end, PIECE)
    ]


def relayed(members):
    return members == 8


def column_of(row):
    return jnp.broadcast_to(row, (128, row.shape[1])).T[:, 0:1]


def row_of(column):
    return jnp.broadcast_to(column, (column.shape[0], 128)).T[0:1]


def pack(doc, guide, offset, width, devices, capacity):
    rows, features = doc.shape
    slots = devices * capacity
    first = isinstance(guide, tuple)
    tail = META if first else 0
    pieces = steps(width)
    rest = [(at, min(PIECE, features - at)) for at in range(width, features, PIECE)] if first else []
    count = len(pieces)

    def kernel(*refs):
        if first:
            home_ref, exponent_ref, doc_ref, out_ref, order_ref, tile, packed, sems = refs
        else:
            order_ref, doc_ref, out_ref, tile, packed, sems = refs
        loads, stores = [], []
        for p, (at, wide) in enumerate(pieces + rest):
            loads.append(
                pltpu.make_async_copy(
                    doc_ref.at[:, pl.ds(offset + at, wide)], tile.at[:, pl.ds(at, wide)], sems.at[p]
                )
            )
            loads[-1].start()

        def send(begin, end):
            piece = pl.ds(begin, end - begin)
            stores.append(
                pltpu.make_async_copy(
                    packed.at[:, piece], out_ref.at[:, piece], sems.at[len(loads) + len(stores)]
                )
            )
            stores[-1].start()

        if first:
            home = home_ref[...].astype(F32)
            target = jnp.floor((home + 0.5) * (1.0 / rows))
            target_col = column_of(target)
            earlier = lax.broadcasted_iota(jnp.int32, (rows, rows), 0) < lax.broadcasted_iota(
                jnp.int32, (rows, rows), 1
            )
            rank = jnp.sum(
                jnp.where(earlier & (target_col == target), 1.0, 0.0), axis=0, keepdims=True
            )
            position = (target * capacity + rank).astype(jnp.int32)
            order = jnp.where(
                lax.broadcasted_iota(jnp.int32, (slots, rows), 0) == position, 1.0, 0.0
            ).astype(BF16)
            order_ref[...] = order
        else:
            order = order_ref[...]
        for p, (at, wide) in enumerate(pieces):
            loads[p].wait()
            packed[:, at : at + wide] = jnp.dot(
                order, tile[:, at : at + wide], preferred_element_type=F32
            ).astype(BF16)
            send(at, at + wide)
        if first:
            for load in loads[count:]:
                load.wait()
            total = jnp.zeros((rows, 128), F32)
            for at in range(0, features, 128):
                values = tile[:, at : at + 128].astype(F32)
                total = total + values * values
            square = row_of(jnp.sum(total, axis=1, keepdims=True))
            inverse = lax.rsqrt(square * (1.0 / features) + EPSILON)
            high = inverse.astype(BF16).astype(F32)
            middle = (inverse - high).astype(BF16).astype(F32)
            slot = home - target * rows
            slot_high = jnp.floor((slot + 0.5) * (1.0 / 32))
            field = lax.broadcasted_iota(jnp.int32, (META, rows), 0)
            meta = jnp.where(field == 0, 1.0, 0.0)
            for f, value in enumerate(
                (
                    slot_high,
                    slot - slot_high * 32,
                    exponent_ref[...].astype(F32),
                    high,
                    middle,
                    inverse - high - middle,
                ),
                1,
            ):
                meta = jnp.where(field == f, value, meta)
            packed[:, width:] = lax.dot_general(
                order, meta.astype(BF16), (((1,), (1,)), ((), ())), preferred_element_type=F32
            ).astype(BF16)
            send(width, width + META)
        for copy in stores:
            copy.wait()

    sent = jax.ShapeDtypeStruct((slots, width + tail), BF16)
    return pl.pallas_call(
        kernel,
        in_specs=[VM, VM, HBM] if first else [VM, HBM],
        out_specs=(HBM, VM) if first else HBM,
        out_shape=(sent, jax.ShapeDtypeStruct((slots, rows), BF16)) if first else sent,
        scratch_shapes=[
            pltpu.VMEM((rows, features if first else width), BF16),
            pltpu.VMEM((slots, width + tail), BF16),
            pltpu.SemaphoreType.DMA((2 * count + len(rest) + 1,)),
        ],
        compiler_params=WHOLE,
        name="pack_first" if first else "pack_next",
    )(*(guide if first else (guide,)), doc)


def unpack(got, order, rows):
    slots, width = got.shape
    first = order is None
    cut = halfway(width)

    def kernel(*refs):
        if first:
            got_ref, own_ref, near_ref, far_ref, order_ref, tile, placed, sems = refs
        else:
            got_ref, order_in, own_ref, near_ref, far_ref, tile, placed, order_ref, sems = refs
            given = pltpu.make_async_copy(order_in, order_ref, sems.at[0])
            given.start()
        begins = [width - META, 0] if first else [0]
        loads = []
        for n, begin in enumerate(begins):
            piece = pl.ds(begin, META if first and n == 0 else width - META * first)
            loads.append(
                pltpu.make_async_copy(got_ref.at[:, piece], tile.at[:, piece], sems.at[1 + n])
            )
            loads[-1].start()
        loads[0].wait()
        if first:
            fields = tile[:, width - META :].astype(F32)
            slot = fields[:, 1:2] * 32 + fields[:, 2:3]
            home = lax.broadcasted_iota(jnp.int32, (slots, rows), 1).astype(F32)
            hit = (home == slot) & (fields[:, 0:1] > 0.5)
            order_ref[...] = jnp.where(hit, 1.0, 0.0).T.astype(BF16)
            loads[1].wait()
        else:
            given.wait()
        stores = []
        for n, (begin, end, ref) in enumerate(((cut, width, far_ref), (0, cut, near_ref))):
            placed[:, begin:end] = jnp.dot(
                order_ref[...], tile[:, begin:end], preferred_element_type=F32
            ).astype(BF16)
            piece = pl.ds(begin, end - begin)
            for m, target in enumerate((ref, own_ref.at[:, piece])):
                stores.append(
                    pltpu.make_async_copy(placed.at[:, piece], target, sems.at[3 + 2 * n + m])
                )
                stores[-1].start()
        for copy in stores:
            copy.wait()

    outs = [jax.ShapeDtypeStruct((rows, columns), BF16) for columns in (width, cut, width - cut)]
    if first:
        outs.append(jax.ShapeDtypeStruct((rows, slots), BF16))
    result = pl.pallas_call(
        kernel,
        in_specs=[HBM] if first else [HBM, HBM],
        out_specs=[HBM] * 3 + [VM] * first,
        out_shape=outs,
        scratch_shapes=[pltpu.VMEM(got.shape, BF16), pltpu.VMEM((rows, width), BF16)]
        + [pltpu.VMEM((rows, slots), BF16)] * (not first)
        + [pltpu.SemaphoreType.DMA((7,))],
        compiler_params=WHOLE,
        name="unpack_first" if first else "unpack_next",
    )(*((got,) if first else (got, order)))
    return result[:3], result[3] if first else order


def runs(member_ref, cluster_ref):
    blocks = cluster_ref.shape[1]
    base = member_ref[0] * B_DEV

    def cluster(index):
        inside = (index >= 0) & (index < blocks)
        return jnp.where(inside, cluster_ref[0, jnp.clip(index, 0, blocks - 1)], -1)

    result = []
    for b in range(B_DEV):
        mine = cluster(base + b)
        back = jnp.where(
            cluster(base + b - 2) == mine, 2, jnp.where(cluster(base + b - 1) == mine, 1, 0)
        )
        links = [
            jnp.where(cluster(base + b - back + k) == mine, 1, 0) for k in range(RUN)
        ]
        result.append((back, links))
    return result


def load_window(member_ref, members, parts, window, sems):
    own, partner, near, far = parts[:4]
    rows, width = own.shape
    cut = halfway(width)
    member = member_ref[0]
    partner_at = pl.multiple_of((1 - member % 2) * 2 * rows, rows)
    other_at = pl.multiple_of((member % 2) * 2 * rows, rows)
    middle = (member == members // 2) | (member == members // 2 - 1)
    second = window.at[pl.ds(other_at, rows), pl.ds(cut, width - cut)]
    copies = [
        pltpu.make_async_copy(source, target, sems.at[n])
        for n, (source, target) in enumerate(
            (
                (own, window.at[pl.ds(rows, rows)]),
                (partner, window.at[pl.ds(partner_at, rows)]),
                (near, window.at[pl.ds(other_at, rows), pl.ds(0, cut)]),
                (far, second),
            )
        )
    ]
    for copy in copies[:3]:
        copy.start()
    if len(parts) == 4:
        copies[3].start()
    else:
        relay = pltpu.make_async_copy(parts[4], second, sems.at[3])
        pl.when(middle)(relay.start)
        pl.when(jnp.logical_not(middle))(copies[3].start)
    return copies


def run_scores(window, back, b, width):
    first = pl.multiple_of((SPAN + b - back) * BLK, BLK)
    return lax.dot_general(
        window[(SPAN + b) * BLK : (SPAN + b + 1) * BLK, 0:width],
        window[pl.ds(first, RUN * BLK), 0:width],
        (((1,), (1,)), ((), ())),
        preferred_element_type=F32,
    )


def partial_scores(member, members, cluster, parts, score):
    rows, width = parts[0].shape
    given = score is not None
    number = len(parts)

    def kernel(member_ref, cluster_ref, *refs):
        if given:
            score_in, score_ref, window, sems = refs[number:]
        else:
            score_ref, factor_ref, window, sems = refs[number:]
        found = runs(member_ref, cluster_ref)
        for copy in load_window(member_ref, members, refs[:number], window, sems):
            copy.wait()
        for b in range(B_DEV):
            value = run_scores(window, found[b][0], b, width if given else width - META)
            score_ref[b] = value + score_in[b] if given else value
        if not given:
            for side in range(3):
                fields = window[side * rows : (side + 1) * rows, width - META :].astype(F32).T
                field = lax.broadcasted_iota(jnp.int32, (8, rows), 0)
                inverse = fields[4:5] + fields[5:6] + fields[6:7]
                factor_ref[side] = jnp.where(field == 0, inverse, jnp.exp2(fields[3:4]))

    score_shape = jax.ShapeDtypeStruct((B_DEV, BLK, RUN * BLK), F32)
    return pl.pallas_call(
        kernel,
        in_specs=[SM, SM] + [HBM] * number + [VM] * given,
        out_shape=score_shape if given else (score_shape, jax.ShapeDtypeStruct((3, 8, rows), F32)),
        scratch_shapes=[
            pltpu.VMEM((3 * rows, width), BF16),
            pltpu.SemaphoreType.DMA((4,)),
        ],
        compiler_params=WHOLE,
        name="partial_scores",
    )(member, cluster, *parts, *([score] if given else []))


def finish(member, members, cluster, chunks, score, factor, features):
    rows = chunks[0][0].shape[0]
    count = len(chunks)
    widths = [chunk[0].shape[1] for chunk in chunks]
    number = len(chunks[0])
    last = count - 1

    def kernel(member_ref, cluster_ref, *refs):
        parts = [refs[number * c : number * (c + 1)] for c in range(count)]
        score_in, factor_in, out_ref, log_ref = refs[number * count : number * count + 4]
        packed, value_ref, factor_ref, early_sems, out_sems, load_sems = refs[
            number * count + 4 : number * count + 10
        ]
        windows = refs[number * count + 10 :]
        found = runs(member_ref, cluster_ref)
        loads = {}

        def load(c):
            loads[c] = load_window(member_ref, members, parts[c], windows[c], load_sems.at[c])

        load(last)
        early = [
            pltpu.make_async_copy(score_in, value_ref, early_sems.at[0]),
            pltpu.make_async_copy(factor_in, factor_ref, early_sems.at[1]),
        ]
        for copy in early:
            copy.start()
        for c in range(last):
            load(c)
        for copy in early:
            copy.wait()
        for copy in loads[last]:
            copy.wait()
        for b in range(B_DEV):
            value_ref[b] += run_scores(windows[last], found[b][0], b, widths[last])
        apart = lax.broadcasted_iota(jnp.int32, (BLK, BLK), 0) - lax.broadcasted_iota(
            jnp.int32, (BLK, BLK), 1
        )
        weights = []
        for b in range(B_DEV):
            back, links = found[b]
            mine = factor_ref[1, :, b * BLK : (b + 1) * BLK]
            row_scale = column_of(mine[0:1]) * features**-0.5
            density = jnp.zeros((BLK, 1), F32)
            tiles = []
            for k in range(RUN):
                block = SPAN + b - back + k
                far = factor_ref[block // B_DEV, :, pl.ds(pl.multiple_of((block % B_DEV) * BLK, BLK), BLK)]
                value = jnp.exp(
                    value_ref[b, :, k * BLK : (k + 1) * BLK] * row_scale * far[0:1] - KERNEL_SHIFT
                )
                kept = (apart + jnp.where(back == k, 0, 2 * BLK) != 0) & (
                    jnp.full((BLK, BLK), links[k], jnp.int32) > 0
                )
                value = jnp.where(kept, value, 0.0)
                density = density + jnp.sum(value, axis=1, keepdims=True)
                tiles.append((value.astype(BF16).astype(F32) * far[1:2]).astype(BF16))
            weights.append(jnp.concatenate(tiles, axis=1))
            log_ref[:, b * BLK : (b + 1) * BLK] = jnp.log(row_of(density))
        outgoing = []
        for c in [last] + list(range(last)):
            if c != last:
                for copy in loads[c]:
                    copy.wait()
            out_at = sum(CHUNKS[:c])
            for at, wide in steps(CHUNKS[c]):
                for b in range(B_DEV):
                    first = pl.multiple_of((SPAN + b - found[b][0]) * BLK, BLK)
                    packed[b * BLK : (b + 1) * BLK, out_at + at : out_at + at + wide] = jnp.dot(
                        weights[b],
                        windows[c][pl.ds(first, RUN * BLK), at : at + wide],
                        preferred_element_type=F32,
                    ).astype(BF16)
                piece = pl.ds(out_at + at, wide)
                copy = pltpu.make_async_copy(
                    packed.at[:, piece], out_ref.at[:, piece], out_sems.at[len(outgoing)]
                )
                copy.start()
                outgoing.append(copy)
        for copy in outgoing:
            copy.wait()

    flat = [ref for chunk in chunks for ref in chunk]
    return pl.pallas_call(
        kernel,
        in_specs=[SM, SM] + [HBM] * (len(flat) + 2),
        out_specs=(HBM, VM),
        out_shape=(
            jax.ShapeDtypeStruct((rows, features), BF16),
            jax.ShapeDtypeStruct((1, rows), F32),
        ),
        scratch_shapes=[
            pltpu.VMEM((rows, features), BF16),
            pltpu.VMEM((B_DEV, BLK, RUN * BLK), F32),
            pltpu.VMEM((3, 8, rows), F32),
            pltpu.SemaphoreType.DMA((2,)),
            pltpu.SemaphoreType.DMA((sum(len(steps(width)) for width in CHUNKS),)),
            pltpu.SemaphoreType.DMA((count, 4)),
        ]
        + [pltpu.VMEM((3 * rows, width), BF16) for width in widths],
        compiler_params=WHOLE,
        name="finish",
    )(member, cluster, *flat, score, factor)


def neighbours(own, near, far, members, beside):
    middle = members // 2
    odd = range(1, members - 1, 2)
    hops = [(i, i + 1) for i in odd] + [(i + 1, i) for i in odd]
    around = [(middle - 1, members - 1), (middle, 0)]
    onward = [(members - 1, middle), (0, middle - 1)]
    apart = [hop for hop in hops if set(hop) != {middle - 1, middle}]
    far = lax.ppermute(far, "member", apart + around if relayed(members) else hops)
    near = lax.ppermute(near, "member", hops)
    partner = lax.ppermute(own, "member", [(i, i ^ 1) for i in range(members)])
    if relayed(members):
        first = far
        if beside:
            first, _ = lax.optimization_barrier((far, partner))
        return (own, partner, near, far, lax.ppermute(first, "member", onward))
    return (own, partner, near, far)


def body(doc_mantissa, doc_exponent, doc_home, block_cluster):
    rows, features = doc_mantissa.shape
    members = lax.axis_size("member")
    devices = lax.axis_size("group") * members
    capacity = rows // devices * 3 // 2
    member = lax.axis_index("member").reshape(1)
    sends = []
    guide = (doc_home[None, :], doc_exponent[None, :])
    for c, width in enumerate(CHUNKS):
        sent = pack(doc_mantissa, guide, sum(CHUNKS[:c]), width, devices, capacity)
        if c == 0:
            sent, guide = sent
        sends.append(sent)

    chunks = []
    order = score = None
    for c in range(len(CHUNKS)):
        if c > 1:
            sends[c], _ = lax.optimization_barrier((sends[c], chunks[c - 2]))
        got = lax.all_to_all(
            sends[c].reshape(devices, capacity, -1), ("group", "member"), 0, 0, tiled=True
        ).reshape(devices * capacity, -1)
        if c > 0:
            got, _ = lax.optimization_barrier((got, chunks[-1]))
        parts, order = unpack(got, order, rows)
        chunks.append(neighbours(*parts, members, c + 1 < len(CHUNKS)))
    for c, chunk in enumerate(chunks[:-1]):
        score = partial_scores(member, members, block_cluster, chunk, score)
        if c == 0:
            score, factor = score
    embed_sum, log_density = finish(
        member, members, block_cluster, chunks, score, factor, features
    )
    return embed_sum, log_density.reshape(rows)


def solution(mesh):
    return jax.shard_map(
        body,
        mesh=mesh,
        in_specs=(
            P(("group", "member"), None),
            P(("group", "member")),
            P(("group", "member")),
            P("group", None),
        ),
        out_specs=(P(("group", "member"), None), P(("group", "member"))),
        check_vma=False,
    )
```

```python
import jax
import jax.numpy as jnp
from jax import lax
from jax.experimental import pallas as pl
from jax.experimental.pallas import tpu as pltpu
from jax.sharding import PartitionSpec as P

BLK = 256
B_DEV = 2
SPAN = 2
RUN = SPAN + 1
WINDOW = B_DEV + 2 * SPAN
META = 128
KERNEL_SHIFT = 4.0
EPSILON = 1e-06
CHUNKS = (1536, 1408, 1152)
PIECE = 768

F32 = jnp.float32
BF16 = jnp.bfloat16
VM = pl.BlockSpec(memory_space=pltpu.VMEM)
SM = pl.BlockSpec(memory_space=pltpu.SMEM)
HBM = pl.BlockSpec(memory_space=pltpu.HBM)
WHOLE = pltpu.CompilerParams(vmem_limit_bytes=64 * 1024 * 1024)


def halfway(width):
    return -(-width // 256) * 128


def steps(width):
    cut = halfway(width)
    return [
        (at, min(PIECE, end - at))
        for begin, end in ((0, cut), (cut, width))
        for at in range(begin, end, PIECE)
    ]


def relayed(members):
    return members == 8


def column_of(row):
    return jnp.broadcast_to(row, (128, row.shape[1])).T[:, 0:1]


def row_of(column):
    return jnp.broadcast_to(column, (column.shape[0], 128)).T[0:1]


def pack(doc, guide, offset, width, devices, capacity):
    rows, features = doc.shape
    slots = devices * capacity
    first = isinstance(guide, tuple)
    tail = META if first else 0
    pieces = steps(width)
    rest = [(at, min(PIECE, features - at)) for at in range(width, features, PIECE)] if first else []
    count = len(pieces)

    def kernel(*refs):
        if first:
            home_ref, exponent_ref, doc_ref, out_ref, order_ref, tile, packed, sems = refs
        else:
            order_ref, doc_ref, out_ref, tile, packed, sems = refs
        loads, stores = [], []
        for p, (at, wide) in enumerate(pieces + rest):
            loads.append(
                pltpu.make_async_copy(
                    doc_ref.at[:, pl.ds(offset + at, wide)], tile.at[:, pl.ds(at, wide)], sems.at[p]
                )
            )
            loads[-1].start()

        def send(begin, end):
            piece = pl.ds(begin, end - begin)
            stores.append(
                pltpu.make_async_copy(
                    packed.at[:, piece], out_ref.at[:, piece], sems.at[len(loads) + len(stores)]
                )
            )
            stores[-1].start()

        if first:
            home = home_ref[...].astype(F32)
            target = jnp.floor((home + 0.5) * (1.0 / rows))
            target_col = column_of(target)
            earlier = lax.broadcasted_iota(jnp.int32, (rows, rows), 0) < lax.broadcasted_iota(
                jnp.int32, (rows, rows), 1
            )
            rank = jnp.sum(
                jnp.where(earlier & (target_col == target), 1.0, 0.0), axis=0, keepdims=True
            )
            position = (target * capacity + rank).astype(jnp.int32)
            order = jnp.where(
                lax.broadcasted_iota(jnp.int32, (slots, rows), 0) == position, 1.0, 0.0
            ).astype(BF16)
            order_ref[...] = order
        else:
            order = order_ref[...]
        for p, (at, wide) in enumerate(pieces):
            loads[p].wait()
            packed[:, at : at + wide] = jnp.dot(
                order, tile[:, at : at + wide], preferred_element_type=F32
            ).astype(BF16)
            send(at, at + wide)
        if first:
            for load in loads[count:]:
                load.wait()
            total = jnp.zeros((rows, 128), F32)
            for at in range(0, features, 128):
                values = tile[:, at : at + 128].astype(F32)
                total = total + values * values
            square = row_of(jnp.sum(total, axis=1, keepdims=True))
            inverse = lax.rsqrt(square * (1.0 / features) + EPSILON)
            high = inverse.astype(BF16).astype(F32)
            middle = (inverse - high).astype(BF16).astype(F32)
            slot = home - target * rows
            slot_high = jnp.floor((slot + 0.5) * (1.0 / 32))
            field = lax.broadcasted_iota(jnp.int32, (META, rows), 0)
            meta = jnp.where(field == 0, 1.0, 0.0)
            for f, value in enumerate(
                (
                    slot_high,
                    slot - slot_high * 32,
                    exponent_ref[...].astype(F32),
                    high,
                    middle,
                    inverse - high - middle,
                ),
                1,
            ):
                meta = jnp.where(field == f, value, meta)
            packed[:, width:] = lax.dot_general(
                order, meta.astype(BF16), (((1,), (1,)), ((), ())), preferred_element_type=F32
            ).astype(BF16)
            send(width, width + META)
        for copy in stores:
            copy.wait()

    sent = jax.ShapeDtypeStruct((slots, width + tail), BF16)
    return pl.pallas_call(
        kernel,
        in_specs=[VM, VM, HBM] if first else [VM, HBM],
        out_specs=(HBM, VM) if first else HBM,
        out_shape=(sent, jax.ShapeDtypeStruct((slots, rows), BF16)) if first else sent,
        scratch_shapes=[
            pltpu.VMEM((rows, features if first else width), BF16),
            pltpu.VMEM((slots, width + tail), BF16),
            pltpu.SemaphoreType.DMA((2 * count + len(rest) + 1,)),
        ],
        compiler_params=WHOLE,
        name="pack_first" if first else "pack_next",
    )(*(guide if first else (guide,)), doc)


def unpack(got, order, rows):
    slots, width = got.shape
    first = order is None
    cut = halfway(width)

    def kernel(*refs):
        if first:
            got_ref, own_ref, near_ref, far_ref, order_ref, tile, placed, sems = refs
        else:
            got_ref, order_in, own_ref, near_ref, far_ref, tile, placed, order_ref, sems = refs
            given = pltpu.make_async_copy(order_in, order_ref, sems.at[0])
            given.start()
        begins = [width - META, 0] if first else [0]
        loads = []
        for n, begin in enumerate(begins):
            piece = pl.ds(begin, META if first and n == 0 else width - META * first)
            loads.append(
                pltpu.make_async_copy(got_ref.at[:, piece], tile.at[:, piece], sems.at[1 + n])
            )
            loads[-1].start()
        loads[0].wait()
        if first:
            fields = tile[:, width - META :].astype(F32)
            slot = fields[:, 1:2] * 32 + fields[:, 2:3]
            home = lax.broadcasted_iota(jnp.int32, (slots, rows), 1).astype(F32)
            hit = (home == slot) & (fields[:, 0:1] > 0.5)
            order_ref[...] = jnp.where(hit, 1.0, 0.0).T.astype(BF16)
            loads[1].wait()
        else:
            given.wait()
        stores = []
        for n, (begin, end, ref) in enumerate(((cut, width, far_ref), (0, cut, near_ref))):
            placed[:, begin:end] = jnp.dot(
                order_ref[...], tile[:, begin:end], preferred_element_type=F32
            ).astype(BF16)
            piece = pl.ds(begin, end - begin)
            for m, target in enumerate((ref, own_ref.at[:, piece])):
                stores.append(
                    pltpu.make_async_copy(placed.at[:, piece], target, sems.at[3 + 2 * n + m])
                )
                stores[-1].start()
        for copy in stores:
            copy.wait()

    outs = [jax.ShapeDtypeStruct((rows, columns), BF16) for columns in (width, cut, width - cut)]
    if first:
        outs.append(jax.ShapeDtypeStruct((rows, slots), BF16))
    result = pl.pallas_call(
        kernel,
        in_specs=[HBM] if first else [HBM, HBM],
        out_specs=[HBM] * 3 + [VM] * first,
        out_shape=outs,
        scratch_shapes=[pltpu.VMEM(got.shape, BF16), pltpu.VMEM((rows, width), BF16)]
        + [pltpu.VMEM((rows, slots), BF16)] * (not first)
        + [pltpu.SemaphoreType.DMA((7,))],
        compiler_params=WHOLE,
        name="unpack_first" if first else "unpack_next",
    )(*((got,) if first else (got, order)))
    return result[:3], result[3] if first else order


def runs(member_ref, cluster_ref):
    blocks = cluster_ref.shape[1]
    base = member_ref[0] * B_DEV

    def cluster(index):
        inside = (index >= 0) & (index < blocks)
        return jnp.where(inside, cluster_ref[0, jnp.clip(index, 0, blocks - 1)], -1)

    result = []
    for b in range(B_DEV):
        mine = cluster(base + b)
        back = jnp.where(
            cluster(base + b - 2) == mine, 2, jnp.where(cluster(base + b - 1) == mine, 1, 0)
        )
        links = [
            jnp.where(cluster(base + b - back + k) == mine, 1, 0) for k in range(RUN)
        ]
        result.append((back, links))
    return result


def load_window(member_ref, members, parts, window, sems):
    own, partner, near, far = parts[:4]
    rows, width = own.shape
    cut = halfway(width)
    member = member_ref[0]
    partner_at = pl.multiple_of((1 - member % 2) * 2 * rows, rows)
    other_at = pl.multiple_of((member % 2) * 2 * rows, rows)
    middle = (member == members // 2) | (member == members // 2 - 1)
    second = window.at[pl.ds(other_at, rows), pl.ds(cut, width - cut)]
    copies = [
        pltpu.make_async_copy(source, target, sems.at[n])
        for n, (source, target) in enumerate(
            (
                (own, window.at[pl.ds(rows, rows)]),
                (partner, window.at[pl.ds(partner_at, rows)]),
                (near, window.at[pl.ds(other_at, rows), pl.ds(0, cut)]),
                (far, second),
            )
        )
    ]
    for copy in copies[:3]:
        copy.start()
    if len(parts) == 4:
        copies[3].start()
    else:
        relay = pltpu.make_async_copy(parts[4], second, sems.at[3])
        pl.when(middle)(relay.start)
        pl.when(jnp.logical_not(middle))(copies[3].start)
    return copies


def run_scores(window, back, b, width):
    first = pl.multiple_of((SPAN + b - back) * BLK, BLK)
    return lax.dot_general(
        window[(SPAN + b) * BLK : (SPAN + b + 1) * BLK, 0:width],
        window[pl.ds(first, RUN * BLK), 0:width],
        (((1,), (1,)), ((), ())),
        preferred_element_type=F32,
    )


def partial_scores(member, members, cluster, parts, score):
    rows, width = parts[0].shape
    given = score is not None
    number = len(parts)

    def kernel(member_ref, cluster_ref, *refs):
        if given:
            score_in, score_ref, window, sems = refs[number:]
        else:
            score_ref, factor_ref, window, sems = refs[number:]
        found = runs(member_ref, cluster_ref)
        for copy in load_window(member_ref, members, refs[:number], window, sems):
            copy.wait()
        for b in range(B_DEV):
            value = run_scores(window, found[b][0], b, width if given else width - META)
            score_ref[b] = value + score_in[b] if given else value
        if not given:
            for side in range(3):
                fields = window[side * rows : (side + 1) * rows, width - META :].astype(F32).T
                field = lax.broadcasted_iota(jnp.int32, (8, rows), 0)
                inverse = fields[4:5] + fields[5:6] + fields[6:7]
                factor_ref[side] = jnp.where(field == 0, inverse, jnp.exp2(fields[3:4]))

    score_shape = jax.ShapeDtypeStruct((B_DEV, BLK, RUN * BLK), F32)
    return pl.pallas_call(
        kernel,
        in_specs=[SM, SM] + [HBM] * number + [VM] * given,
        out_shape=score_shape if given else (score_shape, jax.ShapeDtypeStruct((3, 8, rows), F32)),
        scratch_shapes=[
            pltpu.VMEM((3 * rows, width), BF16),
            pltpu.SemaphoreType.DMA((4,)),
        ],
        compiler_params=WHOLE,
        name="partial_scores",
    )(member, cluster, *parts, *([score] if given else []))


def finish(member, members, cluster, chunks, score, factor, features):
    rows = chunks[0][0].shape[0]
    count = len(chunks)
    widths = [chunk[0].shape[1] for chunk in chunks]
    number = len(chunks[0])
    last = count - 1

    def kernel(member_ref, cluster_ref, *refs):
        parts = [refs[number * c : number * (c + 1)] for c in range(count)]
        score_in, factor_in, out_ref, log_ref = refs[number * count : number * count + 4]
        packed, value_ref, factor_ref, early_sems, out_sems, load_sems = refs[
            number * count + 4 : number * count + 10
        ]
        windows = refs[number * count + 10 :]
        found = runs(member_ref, cluster_ref)
        loads = {}

        def load(c):
            loads[c] = load_window(member_ref, members, parts[c], windows[c], load_sems.at[c])

        load(last)
        early = [
            pltpu.make_async_copy(score_in, value_ref, early_sems.at[0]),
            pltpu.make_async_copy(factor_in, factor_ref, early_sems.at[1]),
        ]
        for copy in early:
            copy.start()
        for c in range(last):
            load(c)
        for copy in early:
            copy.wait()
        for copy in loads[last]:
            copy.wait()
        for b in range(B_DEV):
            value_ref[b] += run_scores(windows[last], found[b][0], b, widths[last])
        apart = lax.broadcasted_iota(jnp.int32, (BLK, BLK), 0) - lax.broadcasted_iota(
            jnp.int32, (BLK, BLK), 1
        )
        weights = []
        for b in range(B_DEV):
            back, links = found[b]
            mine = factor_ref[1, :, b * BLK : (b + 1) * BLK]
            row_scale = column_of(mine[0:1]) * features**-0.5
            density = jnp.zeros((BLK, 1), F32)
            tiles = []
            for k in range(RUN):
                block = SPAN + b - back + k
                far = factor_ref[block // B_DEV, :, pl.ds(pl.multiple_of((block % B_DEV) * BLK, BLK), BLK)]
                value = jnp.exp(
                    value_ref[b, :, k * BLK : (k + 1) * BLK] * row_scale * far[0:1] - KERNEL_SHIFT
                )
                kept = (apart + jnp.where(back == k, 0, 2 * BLK) != 0) & (
                    jnp.full((BLK, BLK), links[k], jnp.int32) > 0
                )
                value = jnp.where(kept, value, 0.0)
                density = density + jnp.sum(value, axis=1, keepdims=True)
                tiles.append((value.astype(BF16).astype(F32) * far[1:2]).astype(BF16))
            weights.append(jnp.concatenate(tiles, axis=1))
            log_ref[:, b * BLK : (b + 1) * BLK] = jnp.log(row_of(density))
        outgoing = []
        for c in [last] + list(range(last)):
            if c != last:
                for copy in loads[c]:
                    copy.wait()
            out_at = sum(CHUNKS[:c])
            for at, wide in steps(CHUNKS[c]):
                for b in range(B_DEV):
                    first = pl.multiple_of((SPAN + b - found[b][0]) * BLK, BLK)
                    packed[b * BLK : (b + 1) * BLK, out_at + at : out_at + at + wide] = jnp.dot(
                        weights[b],
                        windows[c][pl.ds(first, RUN * BLK), at : at + wide],
                        preferred_element_type=F32,
                    ).astype(BF16)
                piece = pl.ds(out_at + at, wide)
                copy = pltpu.make_async_copy(
                    packed.at[:, piece], out_ref.at[:, piece], out_sems.at[len(outgoing)]
                )
                copy.start()
                outgoing.append(copy)
        for copy in outgoing:
            copy.wait()

    flat = [ref for chunk in chunks for ref in chunk]
    return pl.pallas_call(
        kernel,
        in_specs=[SM, SM] + [HBM] * (len(flat) + 2),
        out_specs=(HBM, VM),
        out_shape=(
            jax.ShapeDtypeStruct((rows, features), BF16),
            jax.ShapeDtypeStruct((1, rows), F32),
        ),
        scratch_shapes=[
            pltpu.VMEM((rows, features), BF16),
            pltpu.VMEM((B_DEV, BLK, RUN * BLK), F32),
            pltpu.VMEM((3, 8, rows), F32),
            pltpu.SemaphoreType.DMA((2,)),
            pltpu.SemaphoreType.DMA((sum(len(steps(width)) for width in CHUNKS),)),
            pltpu.SemaphoreType.DMA((count, 4)),
        ]
        + [pltpu.VMEM((3 * rows, width), BF16) for width in widths],
        compiler_params=WHOLE,
        name="finish",
    )(member, cluster, *flat, score, factor)


def neighbours(own, near, far, members, beside):
    middle = members // 2
    odd = range(1, members - 1, 2)
    hops = [(i, i + 1) for i in odd] + [(i + 1, i) for i in odd]
    around = [(middle - 1, members - 1), (middle, 0)]
    onward = [(members - 1, middle), (0, middle - 1)]
    apart = [hop for hop in hops if set(hop) != {middle - 1, middle}]
    far = lax.ppermute(far, "member", apart + around if relayed(members) else hops)
    near = lax.ppermute(near, "member", hops)
    partner = lax.ppermute(own, "member", [(i, i ^ 1) for i in range(members)])
    if relayed(members):
        first = far
        if beside:
            first, _ = lax.optimization_barrier((far, partner))
        return (own, partner, near, far, lax.ppermute(first, "member", onward))
    return (own, partner, near, far)


def body(doc_mantissa, doc_exponent, doc_home, block_cluster):
    rows, features = doc_mantissa.shape
    members = lax.axis_size("member")
    devices = lax.axis_size("group") * members
    capacity = rows // devices * 3 // 2
    member = lax.axis_index("member").reshape(1)
    sends = []
    guide = (doc_home[None, :], doc_exponent[None, :])
    for c, width in enumerate(CHUNKS):
        sent = pack(doc_mantissa, guide, sum(CHUNKS[:c]), width, devices, capacity)
        if c == 0:
            sent, guide = sent
        sends.append(sent)

    chunks = []
    order = score = factor = None

    def scored(c, score):
        found = partial_scores(member, members, block_cluster, chunks[c], score)
        return found if c == 0 else (found, factor)

    for c in range(len(CHUNKS)):
        if c > 1:
            sends[c], _ = lax.optimization_barrier((sends[c], chunks[c - 2]))
            score, factor = scored(c - 2, score)
        got = lax.all_to_all(
            sends[c].reshape(devices, capacity, -1), ("group", "member"), 0, 0, tiled=True
        ).reshape(devices * capacity, -1)
        if c > 0:
            got, *_ = lax.optimization_barrier((got, chunks[-1], score))
        parts, order = unpack(got, order, rows)
        chunks.append(neighbours(*parts, members, c + 1 < len(CHUNKS)))
    score, factor = scored(len(CHUNKS) - 2, score)
    embed_sum, log_density = finish(
        member, members, block_cluster, chunks, score, factor, features
    )
    return embed_sum, log_density.reshape(rows)


def solution(mesh):
    return jax.shard_map(
        body,
        mesh=mesh,
        in_specs=(
            P(("group", "member"), None),
            P(("group", "member")),
            P(("group", "member")),
            P("group", None),
        ),
        out_specs=(P(("group", "member"), None), P(("group", "member"))),
        check_vma=False,
    )
```

```python
import jax
import jax.numpy as jnp
from jax import lax
from jax.experimental import pallas as pl
from jax.experimental.pallas import tpu as pltpu
from jax.sharding import PartitionSpec as P

BLK = 256
B_DEV = 2
SPAN = 2
RUN = SPAN + 1
WINDOW = B_DEV + 2 * SPAN
META = 128
KERNEL_SHIFT = 4.0
EPSILON = 1e-06
CHUNKS = (1408, 1408, 1280)
PIECE = 768

F32 = jnp.float32
BF16 = jnp.bfloat16
VM = pl.BlockSpec(memory_space=pltpu.VMEM)
SM = pl.BlockSpec(memory_space=pltpu.SMEM)
HBM = pl.BlockSpec(memory_space=pltpu.HBM)
WHOLE = pltpu.CompilerParams(vmem_limit_bytes=64 * 1024 * 1024)


def halfway(width):
    return -(-width // 256) * 128


def steps(width):
    cut = halfway(width)
    return [
        (at, min(PIECE, end - at))
        for begin, end in ((0, cut), (cut, width))
        for at in range(begin, end, PIECE)
    ]


def relayed(members):
    return members == 8


def column_of(row):
    return jnp.broadcast_to(row, (128, row.shape[1])).T[:, 0:1]


def row_of(column):
    return jnp.broadcast_to(column, (column.shape[0], 128)).T[0:1]


def pack(doc, guide, offset, width, devices, capacity):
    rows, features = doc.shape
    slots = devices * capacity
    first = isinstance(guide, tuple)
    tail = META if first else 0
    pieces = steps(width)
    rest = [(at, min(PIECE, features - at)) for at in range(width, features, PIECE)] if first else []
    count = len(pieces)

    def kernel(*refs):
        if first:
            home_ref, exponent_ref, doc_ref, out_ref, order_ref, tile, packed, sems = refs
        else:
            order_ref, doc_ref, out_ref, tile, packed, sems = refs
        loads, stores = [], []
        for p, (at, wide) in enumerate(pieces + rest):
            loads.append(
                pltpu.make_async_copy(
                    doc_ref.at[:, pl.ds(offset + at, wide)], tile.at[:, pl.ds(at, wide)], sems.at[p]
                )
            )
            loads[-1].start()

        def send(begin, end):
            piece = pl.ds(begin, end - begin)
            stores.append(
                pltpu.make_async_copy(
                    packed.at[:, piece], out_ref.at[:, piece], sems.at[len(loads) + len(stores)]
                )
            )
            stores[-1].start()

        if first:
            home = home_ref[...].astype(F32)
            target = jnp.floor((home + 0.5) * (1.0 / rows))
            target_col = column_of(target)
            earlier = lax.broadcasted_iota(jnp.int32, (rows, rows), 0) < lax.broadcasted_iota(
                jnp.int32, (rows, rows), 1
            )
            rank = jnp.sum(
                jnp.where(earlier & (target_col == target), 1.0, 0.0), axis=0, keepdims=True
            )
            position = (target * capacity + rank).astype(jnp.int32)
            order = jnp.where(
                lax.broadcasted_iota(jnp.int32, (slots, rows), 0) == position, 1.0, 0.0
            ).astype(BF16)
            order_ref[...] = order
        else:
            order = order_ref[...]
        for p, (at, wide) in enumerate(pieces):
            loads[p].wait()
            packed[:, at : at + wide] = jnp.dot(
                order, tile[:, at : at + wide], preferred_element_type=F32
            ).astype(BF16)
            send(at, at + wide)
        if first:
            for load in loads[count:]:
                load.wait()
            total = jnp.zeros((rows, 128), F32)
            for at in range(0, features, 128):
                values = tile[:, at : at + 128].astype(F32)
                total = total + values * values
            square = row_of(jnp.sum(total, axis=1, keepdims=True))
            inverse = lax.rsqrt(square * (1.0 / features) + EPSILON)
            high = inverse.astype(BF16).astype(F32)
            middle = (inverse - high).astype(BF16).astype(F32)
            slot = home - target * rows
            slot_high = jnp.floor((slot + 0.5) * (1.0 / 32))
            field = lax.broadcasted_iota(jnp.int32, (META, rows), 0)
            meta = jnp.where(field == 0, 1.0, 0.0)
            for f, value in enumerate(
                (
                    slot_high,
                    slot - slot_high * 32,
                    exponent_ref[...].astype(F32),
                    high,
                    middle,
                    inverse - high - middle,
                ),
                1,
            ):
                meta = jnp.where(field == f, value, meta)
            packed[:, width:] = lax.dot_general(
                order, meta.astype(BF16), (((1,), (1,)), ((), ())), preferred_element_type=F32
            ).astype(BF16)
            send(width, width + META)
        for copy in stores:
            copy.wait()

    sent = jax.ShapeDtypeStruct((slots, width + tail), BF16)
    return pl.pallas_call(
        kernel,
        in_specs=[VM, VM, HBM] if first else [VM, HBM],
        out_specs=(HBM, VM) if first else HBM,
        out_shape=(sent, jax.ShapeDtypeStruct((slots, rows), BF16)) if first else sent,
        scratch_shapes=[
            pltpu.VMEM((rows, features if first else width), BF16),
            pltpu.VMEM((slots, width + tail), BF16),
            pltpu.SemaphoreType.DMA((2 * count + len(rest) + 1,)),
        ],
        compiler_params=WHOLE,
        name="pack_first" if first else "pack_next",
    )(*(guide if first else (guide,)), doc)


def unpack(got, order, rows):
    slots, width = got.shape
    first = order is None
    cut = halfway(width)

    def kernel(*refs):
        if first:
            got_ref, own_ref, near_ref, far_ref, order_ref, tile, placed, sems = refs
        else:
            got_ref, order_in, own_ref, near_ref, far_ref, tile, placed, order_ref, sems = refs
            given = pltpu.make_async_copy(order_in, order_ref, sems.at[0])
            given.start()
        begins = [width - META, 0] if first else [0]
        loads = []
        for n, begin in enumerate(begins):
            piece = pl.ds(begin, META if first and n == 0 else width - META * first)
            loads.append(
                pltpu.make_async_copy(got_ref.at[:, piece], tile.at[:, piece], sems.at[1 + n])
            )
            loads[-1].start()
        loads[0].wait()
        if first:
            fields = tile[:, width - META :].astype(F32)
            slot = fields[:, 1:2] * 32 + fields[:, 2:3]
            home = lax.broadcasted_iota(jnp.int32, (slots, rows), 1).astype(F32)
            hit = (home == slot) & (fields[:, 0:1] > 0.5)
            order_ref[...] = jnp.where(hit, 1.0, 0.0).T.astype(BF16)
            loads[1].wait()
        else:
            given.wait()
        stores = []
        for n, (begin, end, ref) in enumerate(((cut, width, far_ref), (0, cut, near_ref))):
            placed[:, begin:end] = jnp.dot(
                order_ref[...], tile[:, begin:end], preferred_element_type=F32
            ).astype(BF16)
            piece = pl.ds(begin, end - begin)
            for m, target in enumerate((ref, own_ref.at[:, piece])):
                stores.append(
                    pltpu.make_async_copy(placed.at[:, piece], target, sems.at[3 + 2 * n + m])
                )
                stores[-1].start()
        for copy in stores:
            copy.wait()

    outs = [jax.ShapeDtypeStruct((rows, columns), BF16) for columns in (width, cut, width - cut)]
    if first:
        outs.append(jax.ShapeDtypeStruct((rows, slots), BF16))
    result = pl.pallas_call(
        kernel,
        in_specs=[HBM] if first else [HBM, HBM],
        out_specs=[HBM] * 3 + [VM] * first,
        out_shape=outs,
        scratch_shapes=[pltpu.VMEM(got.shape, BF16), pltpu.VMEM((rows, width), BF16)]
        + [pltpu.VMEM((rows, slots), BF16)] * (not first)
        + [pltpu.SemaphoreType.DMA((7,))],
        compiler_params=WHOLE,
        name="unpack_first" if first else "unpack_next",
    )(*((got,) if first else (got, order)))
    return result[:3], result[3] if first else order


def runs(member_ref, cluster_ref):
    blocks = cluster_ref.shape[1]
    base = member_ref[0] * B_DEV

    def cluster(index):
        inside = (index >= 0) & (index < blocks)
        return jnp.where(inside, cluster_ref[0, jnp.clip(index, 0, blocks - 1)], -1)

    result = []
    for b in range(B_DEV):
        mine = cluster(base + b)
        back = jnp.where(
            cluster(base + b - 2) == mine, 2, jnp.where(cluster(base + b - 1) == mine, 1, 0)
        )
        links = [
            jnp.where(cluster(base + b - back + k) == mine, 1, 0) for k in range(RUN)
        ]
        result.append((back, links))
    return result


def load_window(member_ref, members, parts, window, sems):
    own, partner, near, far = parts[:4]
    rows, width = own.shape
    cut = halfway(width)
    member = member_ref[0]
    partner_at = pl.multiple_of((1 - member % 2) * 2 * rows, rows)
    other_at = pl.multiple_of((member % 2) * 2 * rows, rows)
    middle = (member == members // 2) | (member == members // 2 - 1)
    second = window.at[pl.ds(other_at, rows), pl.ds(cut, width - cut)]
    copies = [
        pltpu.make_async_copy(source, target, sems.at[n])
        for n, (source, target) in enumerate(
            (
                (own, window.at[pl.ds(rows, rows)]),
                (partner, window.at[pl.ds(partner_at, rows)]),
                (near, window.at[pl.ds(other_at, rows), pl.ds(0, cut)]),
                (far, second),
            )
        )
    ]
    for copy in copies[:3]:
        copy.start()
    if len(parts) == 4:
        copies[3].start()
    else:
        relay = pltpu.make_async_copy(parts[4], second, sems.at[3])
        pl.when(middle)(relay.start)
        pl.when(jnp.logical_not(middle))(copies[3].start)
    return copies


def run_scores(window, back, b, width):
    first = pl.multiple_of((SPAN + b - back) * BLK, BLK)
    return lax.dot_general(
        window[(SPAN + b) * BLK : (SPAN + b + 1) * BLK, 0:width],
        window[pl.ds(first, RUN * BLK), 0:width],
        (((1,), (1,)), ((), ())),
        preferred_element_type=F32,
    )


def partial_scores(member, members, cluster, parts, score):
    rows, width = parts[0].shape
    given = score is not None
    number = len(parts)

    def kernel(member_ref, cluster_ref, *refs):
        if given:
            score_in, score_ref, window, sems = refs[number:]
        else:
            score_ref, factor_ref, window, sems = refs[number:]
        found = runs(member_ref, cluster_ref)
        for copy in load_window(member_ref, members, refs[:number], window, sems):
            copy.wait()
        for b in range(B_DEV):
            value = run_scores(window, found[b][0], b, width if given else width - META)
            score_ref[b] = value + score_in[b] if given else value
        if not given:
            for side in range(3):
                fields = window[side * rows : (side + 1) * rows, width - META :].astype(F32).T
                field = lax.broadcasted_iota(jnp.int32, (8, rows), 0)
                inverse = fields[4:5] + fields[5:6] + fields[6:7]
                factor_ref[side] = jnp.where(field == 0, inverse, jnp.exp2(fields[3:4]))

    score_shape = jax.ShapeDtypeStruct((B_DEV, BLK, RUN * BLK), F32)
    return pl.pallas_call(
        kernel,
        in_specs=[SM, SM] + [HBM] * number + [VM] * given,
        out_shape=score_shape if given else (score_shape, jax.ShapeDtypeStruct((3, 8, rows), F32)),
        scratch_shapes=[
            pltpu.VMEM((3 * rows, width), BF16),
            pltpu.SemaphoreType.DMA((4,)),
        ],
        compiler_params=WHOLE,
        name="partial_scores",
    )(member, cluster, *parts, *([score] if given else []))


def finish(member, members, cluster, chunks, score, factor, features):
    rows = chunks[0][0].shape[0]
    count = len(chunks)
    widths = [chunk[0].shape[1] for chunk in chunks]
    number = len(chunks[0])
    last = count - 1

    def kernel(member_ref, cluster_ref, *refs):
        parts = [refs[number * c : number * (c + 1)] for c in range(count)]
        score_in, factor_in, out_ref, log_ref = refs[number * count : number * count + 4]
        packed, value_ref, factor_ref, early_sems, out_sems, load_sems = refs[
            number * count + 4 : number * count + 10
        ]
        windows = refs[number * count + 10 :]
        found = runs(member_ref, cluster_ref)
        loads = {}

        def load(c):
            loads[c] = load_window(member_ref, members, parts[c], windows[c], load_sems.at[c])

        load(last)
        early = [
            pltpu.make_async_copy(score_in, value_ref, early_sems.at[0]),
            pltpu.make_async_copy(factor_in, factor_ref, early_sems.at[1]),
        ]
        for copy in early:
            copy.start()
        for c in range(last):
            load(c)
        for copy in early:
            copy.wait()
        for copy in loads[last]:
            copy.wait()
        for b in range(B_DEV):
            value_ref[b] += run_scores(windows[last], found[b][0], b, widths[last])
        apart = lax.broadcasted_iota(jnp.int32, (BLK, BLK), 0) - lax.broadcasted_iota(
            jnp.int32, (BLK, BLK), 1
        )
        weights = []
        for b in range(B_DEV):
            back, links = found[b]
            mine = factor_ref[1, :, b * BLK : (b + 1) * BLK]
            row_scale = column_of(mine[0:1]) * features**-0.5
            density = jnp.zeros((BLK, 1), F32)
            tiles = []
            for k in range(RUN):
                block = SPAN + b - back + k
                far = factor_ref[block // B_DEV, :, pl.ds(pl.multiple_of((block % B_DEV) * BLK, BLK), BLK)]
                value = jnp.exp(
                    value_ref[b, :, k * BLK : (k + 1) * BLK] * row_scale * far[0:1] - KERNEL_SHIFT
                )
                kept = (apart + jnp.where(back == k, 0, 2 * BLK) != 0) & (
                    jnp.full((BLK, BLK), links[k], jnp.int32) > 0
                )
                value = jnp.where(kept, value, 0.0)
                density = density + jnp.sum(value, axis=1, keepdims=True)
                tiles.append((value.astype(BF16).astype(F32) * far[1:2]).astype(BF16))
            weights.append(jnp.concatenate(tiles, axis=1))
            log_ref[:, b * BLK : (b + 1) * BLK] = jnp.log(row_of(density))
        outgoing = []
        for c in [last] + list(range(last)):
            if c != last:
                for copy in loads[c]:
                    copy.wait()
            out_at = sum(CHUNKS[:c])
            for at, wide in steps(CHUNKS[c]):
                for b in range(B_DEV):
                    first = pl.multiple_of((SPAN + b - found[b][0]) * BLK, BLK)
                    packed[b * BLK : (b + 1) * BLK, out_at + at : out_at + at + wide] = jnp.dot(
                        weights[b],
                        windows[c][pl.ds(first, RUN * BLK), at : at + wide],
                        preferred_element_type=F32,
                    ).astype(BF16)
                piece = pl.ds(out_at + at, wide)
                copy = pltpu.make_async_copy(
                    packed.at[:, piece], out_ref.at[:, piece], out_sems.at[len(outgoing)]
                )
                copy.start()
                outgoing.append(copy)
        for copy in outgoing:
            copy.wait()

    flat = [ref for chunk in chunks for ref in chunk]
    return pl.pallas_call(
        kernel,
        in_specs=[SM, SM] + [HBM] * (len(flat) + 2),
        out_specs=(HBM, VM),
        out_shape=(
            jax.ShapeDtypeStruct((rows, features), BF16),
            jax.ShapeDtypeStruct((1, rows), F32),
        ),
        scratch_shapes=[
            pltpu.VMEM((rows, features), BF16),
            pltpu.VMEM((B_DEV, BLK, RUN * BLK), F32),
            pltpu.VMEM((3, 8, rows), F32),
            pltpu.SemaphoreType.DMA((2,)),
            pltpu.SemaphoreType.DMA((sum(len(steps(width)) for width in CHUNKS),)),
            pltpu.SemaphoreType.DMA((count, 4)),
        ]
        + [pltpu.VMEM((3 * rows, width), BF16) for width in widths],
        compiler_params=WHOLE,
        name="finish",
    )(member, cluster, *flat, score, factor)


def neighbours(own, near, far, members, beside):
    middle = members // 2
    odd = range(1, members - 1, 2)
    hops = [(i, i + 1) for i in odd] + [(i + 1, i) for i in odd]
    around = [(middle - 1, members - 1), (middle, 0)]
    onward = [(members - 1, middle), (0, middle - 1)]
    apart = [hop for hop in hops if set(hop) != {middle - 1, middle}]
    far = lax.ppermute(far, "member", apart + around if relayed(members) else hops)
    near = lax.ppermute(near, "member", hops)
    partner = lax.ppermute(own, "member", [(i, i ^ 1) for i in range(members)])
    if relayed(members):
        first = far
        if beside:
            first, _ = lax.optimization_barrier((far, partner))
        return (own, partner, near, far, lax.ppermute(first, "member", onward))
    return (own, partner, near, far)


def body(doc_mantissa, doc_exponent, doc_home, block_cluster):
    rows, features = doc_mantissa.shape
    members = lax.axis_size("member")
    devices = lax.axis_size("group") * members
    capacity = rows // devices * 3 // 2
    member = lax.axis_index("member").reshape(1)
    sends = []
    guide = (doc_home[None, :], doc_exponent[None, :])
    for c, width in enumerate(CHUNKS):
        sent = pack(doc_mantissa, guide, sum(CHUNKS[:c]), width, devices, capacity)
        if c == 0:
            sent, guide = sent
        sends.append(sent)

    chunks = []
    order = score = factor = None

    def scored(c, score):
        found = partial_scores(member, members, block_cluster, chunks[c], score)
        return found if c == 0 else (found, factor)

    for c in range(len(CHUNKS)):
        if c > 1:
            sends[c], _ = lax.optimization_barrier((sends[c], chunks[c - 2]))
            score, factor = scored(c - 2, score)
        got = lax.all_to_all(
            sends[c].reshape(devices, capacity, -1), ("group", "member"), 0, 0, tiled=True
        ).reshape(devices * capacity, -1)
        if c > 0:
            got, *_ = lax.optimization_barrier((got, chunks[-1], score))
        parts, order = unpack(got, order, rows)
        chunks.append(neighbours(*parts, members, c + 1 < len(CHUNKS)))
    score, factor = scored(len(CHUNKS) - 2, score)
    embed_sum, log_density = finish(
        member, members, block_cluster, chunks, score, factor, features
    )
    return embed_sum, log_density.reshape(rows)


def solution(mesh):
    return jax.shard_map(
        body,
        mesh=mesh,
        in_specs=(
            P(("group", "member"), None),
            P(("group", "member")),
            P(("group", "member")),
            P("group", None),
        ),
        out_specs=(P(("group", "member"), None), P(("group", "member"))),
        check_vma=False,
    )
```

```python
import jax
import jax.numpy as jnp
from jax import lax
from jax.experimental import pallas as pl
from jax.experimental.pallas import tpu as pltpu
from jax.sharding import PartitionSpec as P

BLK = 256
B_DEV = 2
SPAN = 2
RUN = SPAN + 1
WINDOW = B_DEV + 2 * SPAN
META = 128
KERNEL_SHIFT = 4.0
EPSILON = 1e-06
CHUNKS = (1408, 1408, 1280)
PIECE = 768

F32 = jnp.float32
BF16 = jnp.bfloat16
VM = pl.BlockSpec(memory_space=pltpu.VMEM)
SM = pl.BlockSpec(memory_space=pltpu.SMEM)
HBM = pl.BlockSpec(memory_space=pltpu.HBM)
WHOLE = pltpu.CompilerParams(vmem_limit_bytes=64 * 1024 * 1024)


def halfway(width):
    return -(-width // 256) * 128


def steps(width):
    cut = halfway(width)
    return [
        (at, min(PIECE, end - at))
        for begin, end in ((0, cut), (cut, width))
        for at in range(begin, end, PIECE)
    ]


def relayed(members):
    return members == 8


def column_of(row):
    return jnp.broadcast_to(row, (128, row.shape[1])).T[:, 0:1]


def row_of(column):
    return jnp.broadcast_to(column, (column.shape[0], 128)).T[0:1]


def pack(doc, guide, offset, width, devices, capacity):
    rows, features = doc.shape
    slots = devices * capacity
    first = isinstance(guide, tuple)
    tail = META if first else 0
    pieces = steps(width)
    rest = [(at, min(PIECE, features - at)) for at in range(width, features, PIECE)] if first else []
    count = len(pieces)

    def kernel(*refs):
        if first:
            home_ref, exponent_ref, doc_ref, out_ref, order_ref, tile, packed, sems = refs
        else:
            order_ref, doc_ref, out_ref, tile, packed, sems = refs
        loads, stores = [], []
        for p, (at, wide) in enumerate(pieces + rest):
            loads.append(
                pltpu.make_async_copy(
                    doc_ref.at[:, pl.ds(offset + at, wide)], tile.at[:, pl.ds(at, wide)], sems.at[p]
                )
            )
            loads[-1].start()

        def send(begin, end):
            piece = pl.ds(begin, end - begin)
            stores.append(
                pltpu.make_async_copy(
                    packed.at[:, piece], out_ref.at[:, piece], sems.at[len(loads) + len(stores)]
                )
            )
            stores[-1].start()

        if first:
            home = home_ref[...].astype(F32)
            target = jnp.floor((home + 0.5) * (1.0 / rows))
            target_col = column_of(target)
            earlier = lax.broadcasted_iota(jnp.int32, (rows, rows), 0) < lax.broadcasted_iota(
                jnp.int32, (rows, rows), 1
            )
            rank = jnp.sum(
                jnp.where(earlier & (target_col == target), 1.0, 0.0), axis=0, keepdims=True
            )
            position = (target * capacity + rank).astype(jnp.int32)
            order = jnp.where(
                lax.broadcasted_iota(jnp.int32, (slots, rows), 0) == position, 1.0, 0.0
            ).astype(BF16)
            order_ref[...] = order
        else:
            order = order_ref[...]
        total = jnp.zeros((rows, 128), F32)
        for p, (at, wide) in enumerate(pieces):
            loads[p].wait()
            end = at + wide
            if first and p + 1 == count:
                for load in loads[count:]:
                    load.wait()
                end = features
            packed[:, at : at + wide] = jnp.dot(
                order, tile[:, at : at + wide], preferred_element_type=F32
            ).astype(BF16)
            if first:
                for column in range(at, end, 128):
                    values = tile[:, column : column + 128].astype(F32)
                    total = total + values * values
            send(at, at + wide)
        if first:
            square = row_of(jnp.sum(total, axis=1, keepdims=True))
            inverse = lax.rsqrt(square * (1.0 / features) + EPSILON)
            high = inverse.astype(BF16).astype(F32)
            middle = (inverse - high).astype(BF16).astype(F32)
            slot = home - target * rows
            slot_high = jnp.floor((slot + 0.5) * (1.0 / 32))
            field = lax.broadcasted_iota(jnp.int32, (META, rows), 0)
            meta = jnp.where(field == 0, 1.0, 0.0)
            for f, value in enumerate(
                (
                    slot_high,
                    slot - slot_high * 32,
                    exponent_ref[...].astype(F32),
                    high,
                    middle,
                    inverse - high - middle,
                ),
                1,
            ):
                meta = jnp.where(field == f, value, meta)
            packed[:, width:] = lax.dot_general(
                order, meta.astype(BF16), (((1,), (1,)), ((), ())), preferred_element_type=F32
            ).astype(BF16)
            send(width, width + META)
        for copy in stores:
            copy.wait()

    sent = jax.ShapeDtypeStruct((slots, width + tail), BF16)
    return pl.pallas_call(
        kernel,
        in_specs=[VM, VM, HBM] if first else [VM, HBM],
        out_specs=(HBM, VM) if first else HBM,
        out_shape=(sent, jax.ShapeDtypeStruct((slots, rows), BF16)) if first else sent,
        scratch_shapes=[
            pltpu.VMEM((rows, features if first else width), BF16),
            pltpu.VMEM((slots, width + tail), BF16),
            pltpu.SemaphoreType.DMA((2 * count + len(rest) + 1,)),
        ],
        compiler_params=WHOLE,
        name="pack_first" if first else "pack_next",
    )(*(guide if first else (guide,)), doc)


def unpack(got, order, rows):
    slots, width = got.shape
    first = order is None
    cut = halfway(width)

    def kernel(*refs):
        if first:
            got_ref, own_ref, near_ref, far_ref, order_ref, tile, placed, sems = refs
        else:
            got_ref, order_in, own_ref, near_ref, far_ref, tile, placed, order_ref, sems = refs
            given = pltpu.make_async_copy(order_in, order_ref, sems.at[0])
            given.start()
        begins = [width - META, 0] if first else [0]
        loads = []
        for n, begin in enumerate(begins):
            piece = pl.ds(begin, META if first and n == 0 else width - META * first)
            loads.append(
                pltpu.make_async_copy(got_ref.at[:, piece], tile.at[:, piece], sems.at[1 + n])
            )
            loads[-1].start()
        loads[0].wait()
        if first:
            fields = tile[:, width - META :].astype(F32)
            slot = fields[:, 1:2] * 32 + fields[:, 2:3]
            home = lax.broadcasted_iota(jnp.int32, (slots, rows), 1).astype(F32)
            hit = (home == slot) & (fields[:, 0:1] > 0.5)
            order_ref[...] = jnp.where(hit, 1.0, 0.0).T.astype(BF16)
            loads[1].wait()
        else:
            given.wait()
        stores = []
        for n, (begin, end, ref) in enumerate(((cut, width, far_ref), (0, cut, near_ref))):
            placed[:, begin:end] = jnp.dot(
                order_ref[...], tile[:, begin:end], preferred_element_type=F32
            ).astype(BF16)
            piece = pl.ds(begin, end - begin)
            for m, target in enumerate((ref, own_ref.at[:, piece])):
                stores.append(
                    pltpu.make_async_copy(placed.at[:, piece], target, sems.at[3 + 2 * n + m])
                )
                stores[-1].start()
        for copy in stores:
            copy.wait()

    outs = [jax.ShapeDtypeStruct((rows, columns), BF16) for columns in (width, cut, width - cut)]
    if first:
        outs.append(jax.ShapeDtypeStruct((rows, slots), BF16))
    result = pl.pallas_call(
        kernel,
        in_specs=[HBM] if first else [HBM, HBM],
        out_specs=[HBM] * 3 + [VM] * first,
        out_shape=outs,
        scratch_shapes=[pltpu.VMEM(got.shape, BF16), pltpu.VMEM((rows, width), BF16)]
        + [pltpu.VMEM((rows, slots), BF16)] * (not first)
        + [pltpu.SemaphoreType.DMA((7,))],
        compiler_params=WHOLE,
        name="unpack_first" if first else "unpack_next",
    )(*((got,) if first else (got, order)))
    return result[:3], result[3] if first else order


def runs(member_ref, cluster_ref):
    blocks = cluster_ref.shape[1]
    base = member_ref[0] * B_DEV

    def cluster(index):
        inside = (index >= 0) & (index < blocks)
        return jnp.where(inside, cluster_ref[0, jnp.clip(index, 0, blocks - 1)], -1)

    result = []
    for b in range(B_DEV):
        mine = cluster(base + b)
        back = jnp.where(
            cluster(base + b - 2) == mine, 2, jnp.where(cluster(base + b - 1) == mine, 1, 0)
        )
        links = [
            jnp.where(cluster(base + b - back + k) == mine, 1, 0) for k in range(RUN)
        ]
        result.append((back, links))
    return result


def load_window(member_ref, members, parts, window, sems, half):
    own, partner = parts[:2]
    rows, width = own.shape
    cut = halfway(width)
    member = member_ref[0]
    partner_at = pl.multiple_of((1 - member % 2) * 2 * rows, rows)
    other_at = pl.multiple_of((member % 2) * 2 * rows, rows)
    middle = (member == members // 2) | (member == members // 2 - 1)
    columns = pl.ds(half * cut, width - cut if half else cut)
    other = window.at[pl.ds(other_at, rows), columns]
    copies = [
        pltpu.make_async_copy(source, target, sems.at[3 * half + n])
        for n, (source, target) in enumerate(
            (
                (own.at[:, columns], window.at[pl.ds(rows, rows), columns]),
                (partner.at[:, columns], window.at[pl.ds(partner_at, rows), columns]),
                (parts[2 + half], other),
            )
        )
    ]
    copies[0].start()
    copies[1].start()
    if half == 0 or len(parts) == 4:
        copies[2].start()
    else:
        relay = pltpu.make_async_copy(parts[4], other, sems.at[3 * half + 2])
        pl.when(middle)(relay.start)
        pl.when(jnp.logical_not(middle))(copies[2].start)
    return copies


def run_scores(window, back, b, column, end):
    first = pl.multiple_of((SPAN + b - back) * BLK, BLK)
    return lax.dot_general(
        window[(SPAN + b) * BLK : (SPAN + b + 1) * BLK, column:end],
        window[pl.ds(first, RUN * BLK), column:end],
        (((1,), (1,)), ((), ())),
        preferred_element_type=F32,
    )


def partial_scores(member, members, cluster, parts, score):
    rows, width = parts[0].shape
    given = score is not None
    number = len(parts)

    def kernel(member_ref, cluster_ref, *refs):
        if given:
            score_in, score_ref, window, sems = refs[number:]
        else:
            score_ref, factor_ref, window, sems = refs[number:]
        found = runs(member_ref, cluster_ref)
        halves = [
            load_window(member_ref, members, refs[:number], window, sems, half) for half in (0, 1)
        ]
        for copy in halves[0] + halves[1]:
            copy.wait()
        for b in range(B_DEV):
            value = run_scores(window, found[b][0], b, 0, width if given else width - META)
            score_ref[b] = value + score_in[b] if given else value
        if not given:
            for side in range(3):
                fields = window[side * rows : (side + 1) * rows, width - META :].astype(F32).T
                field = lax.broadcasted_iota(jnp.int32, (8, rows), 0)
                inverse = fields[4:5] + fields[5:6] + fields[6:7]
                factor_ref[side] = jnp.where(field == 0, inverse, jnp.exp2(fields[3:4]))

    score_shape = jax.ShapeDtypeStruct((B_DEV, BLK, RUN * BLK), F32)
    return pl.pallas_call(
        kernel,
        in_specs=[SM, SM] + [HBM] * number + [VM] * given,
        out_shape=score_shape if given else (score_shape, jax.ShapeDtypeStruct((3, 8, rows), F32)),
        scratch_shapes=[
            pltpu.VMEM((3 * rows, width), BF16),
            pltpu.SemaphoreType.DMA((6,)),
        ],
        compiler_params=WHOLE,
        name="partial_scores",
    )(member, cluster, *parts, *([score] if given else []))


def finish(member, members, cluster, chunks, score, factor, features):
    rows = chunks[0][0].shape[0]
    count = len(chunks)
    widths = [chunk[0].shape[1] for chunk in chunks]
    number = len(chunks[0])
    last = count - 1

    def kernel(member_ref, cluster_ref, *refs):
        parts = [refs[number * c : number * (c + 1)] for c in range(count)]
        score_in, factor_in, out_ref, log_ref = refs[number * count : number * count + 4]
        packed, value_ref, factor_ref, early_sems, out_sems, load_sems = refs[
            number * count + 4 : number * count + 10
        ]
        windows = refs[number * count + 10 :]
        found = runs(member_ref, cluster_ref)
        loads = {}

        def load(c, half):
            copies = load_window(member_ref, members, parts[c], windows[c], load_sems.at[c], half)
            loads.setdefault(c, []).append(copies)

        load(last, 0)
        early = [
            pltpu.make_async_copy(score_in, value_ref, early_sems.at[0]),
            pltpu.make_async_copy(factor_in, factor_ref, early_sems.at[1]),
        ]
        for copy in early:
            copy.start()
        load(last, 1)
        cut = halfway(widths[last])
        for half, (column, end) in enumerate(((0, cut), (cut, widths[last]))):
            for copy in loads[last][half] + (early if half == 0 else []):
                copy.wait()
            for c in reversed(range(last)):
                if (c == last - 1) == (half == 0):
                    load(c, 0)
                    load(c, 1)
            for b in range(B_DEV):
                value_ref[b] += run_scores(windows[last], found[b][0], b, column, end)
        apart = lax.broadcasted_iota(jnp.int32, (BLK, BLK), 0) - lax.broadcasted_iota(
            jnp.int32, (BLK, BLK), 1
        )
        weights = []
        for b in range(B_DEV):
            back, links = found[b]
            mine = factor_ref[1, :, b * BLK : (b + 1) * BLK]
            row_scale = column_of(mine[0:1]) * features**-0.5
            density = jnp.zeros((BLK, 1), F32)
            tiles = []
            for k in range(RUN):
                block = SPAN + b - back + k
                far = factor_ref[block // B_DEV, :, pl.ds(pl.multiple_of((block % B_DEV) * BLK, BLK), BLK)]
                value = jnp.exp(
                    value_ref[b, :, k * BLK : (k + 1) * BLK] * row_scale * far[0:1] - KERNEL_SHIFT
                )
                kept = (apart + jnp.where(back == k, 0, 2 * BLK) != 0) & (
                    jnp.full((BLK, BLK), links[k], jnp.int32) > 0
                )
                value = jnp.where(kept, value, 0.0)
                density = density + jnp.sum(value, axis=1, keepdims=True)
                tiles.append((value.astype(BF16).astype(F32) * far[1:2]).astype(BF16))
            weights.append(jnp.concatenate(tiles, axis=1))
            log_ref[:, b * BLK : (b + 1) * BLK] = jnp.log(row_of(density))
        outgoing = []
        for c in reversed(range(count)):
            if c != last:
                for copy in loads[c][0] + loads[c][1]:
                    copy.wait()
            out_at = sum(CHUNKS[:c])
            for at, wide in steps(CHUNKS[c]):
                for b in range(B_DEV):
                    first = pl.multiple_of((SPAN + b - found[b][0]) * BLK, BLK)
                    packed[b * BLK : (b + 1) * BLK, out_at + at : out_at + at + wide] = jnp.dot(
                        weights[b],
                        windows[c][pl.ds(first, RUN * BLK), at : at + wide],
                        preferred_element_type=F32,
                    ).astype(BF16)
                piece = pl.ds(out_at + at, wide)
                copy = pltpu.make_async_copy(
                    packed.at[:, piece], out_ref.at[:, piece], out_sems.at[len(outgoing)]
                )
                copy.start()
                outgoing.append(copy)
        for copy in outgoing:
            copy.wait()

    flat = [ref for chunk in chunks for ref in chunk]
    return pl.pallas_call(
        kernel,
        in_specs=[SM, SM] + [HBM] * (len(flat) + 2),
        out_specs=(HBM, VM),
        out_shape=(
            jax.ShapeDtypeStruct((rows, features), BF16),
            jax.ShapeDtypeStruct((1, rows), F32),
        ),
        scratch_shapes=[
            pltpu.VMEM((rows, features), BF16),
            pltpu.VMEM((B_DEV, BLK, RUN * BLK), F32),
            pltpu.VMEM((3, 8, rows), F32),
            pltpu.SemaphoreType.DMA((2,)),
            pltpu.SemaphoreType.DMA((sum(len(steps(width)) for width in CHUNKS),)),
            pltpu.SemaphoreType.DMA((count, 6)),
        ]
        + [pltpu.VMEM((3 * rows, width), BF16) for width in widths],
        compiler_params=WHOLE,
        name="finish",
    )(member, cluster, *flat, score, factor)


def neighbours(own, near, far, members, beside):
    middle = members // 2
    odd = range(1, members - 1, 2)
    hops = [(i, i + 1) for i in odd] + [(i + 1, i) for i in odd]
    around = [(middle - 1, members - 1), (middle, 0)]
    onward = [(members - 1, middle), (0, middle - 1)]
    apart = [hop for hop in hops if set(hop) != {middle - 1, middle}]
    far = lax.ppermute(far, "member", apart + around if relayed(members) else hops)
    near = lax.ppermute(near, "member", hops)
    partner = lax.ppermute(own, "member", [(i, i ^ 1) for i in range(members)])
    if relayed(members):
        first = far
        if beside:
            first, _ = lax.optimization_barrier((far, partner))
        return (own, partner, near, far, lax.ppermute(first, "member", onward))
    return (own, partner, near, far)


def body(doc_mantissa, doc_exponent, doc_home, block_cluster):
    rows, features = doc_mantissa.shape
    members = lax.axis_size("member")
    devices = lax.axis_size("group") * members
    capacity = rows // devices * 3 // 2
    member = lax.axis_index("member").reshape(1)
    sends = []
    guide = (doc_home[None, :], doc_exponent[None, :])
    for c, width in enumerate(CHUNKS):
        sent = pack(doc_mantissa, guide, sum(CHUNKS[:c]), width, devices, capacity)
        if c == 0:
            sent, guide = sent
        sends.append(sent)

    chunks = []
    order = score = factor = None

    def scored(c, score):
        found = partial_scores(member, members, block_cluster, chunks[c], score)
        return found if c == 0 else (found, factor)

    for c in range(len(CHUNKS)):
        if c > 1:
            sends[c], _ = lax.optimization_barrier((sends[c], chunks[c - 2]))
            score, factor = scored(c - 2, score)
        got = lax.all_to_all(
            sends[c].reshape(devices, capacity, -1), ("group", "member"), 0, 0, tiled=True
        ).reshape(devices * capacity, -1)
        if c > 0:
            got, *_ = lax.optimization_barrier((got, chunks[-1], score))
        parts, order = unpack(got, order, rows)
        chunks.append(neighbours(*parts, members, c + 1 < len(CHUNKS)))
    score, factor = scored(len(CHUNKS) - 2, score)
    embed_sum, log_density = finish(
        member, members, block_cluster, chunks, score, factor, features
    )
    return embed_sum, log_density.reshape(rows)


def solution(mesh):
    return jax.shard_map(
        body,
        mesh=mesh,
        in_specs=(
            P(("group", "member"), None),
            P(("group", "member")),
            P(("group", "member")),
            P("group", None),
        ),
        out_specs=(P(("group", "member"), None), P(("group", "member"))),
        check_vma=False,
    )
```

```python
import jax
import jax.numpy as jnp
from jax import lax
from jax.experimental import pallas as pl
from jax.experimental.pallas import tpu as pltpu
from jax.sharding import PartitionSpec as P

BLK = 256
B_DEV = 2
SPAN = 2
RUN = SPAN + 1
WINDOW = B_DEV + 2 * SPAN
META = 128
KERNEL_SHIFT = 4.0
EPSILON = 1e-06
CHUNKS = (1408, 1408, 1280)
PIECE = 768
NEAR = {CHUNKS[0] + META: 896}

F32 = jnp.float32
BF16 = jnp.bfloat16
VM = pl.BlockSpec(memory_space=pltpu.VMEM)
SM = pl.BlockSpec(memory_space=pltpu.SMEM)
HBM = pl.BlockSpec(memory_space=pltpu.HBM)
WHOLE = pltpu.CompilerParams(vmem_limit_bytes=64 * 1024 * 1024)


def halfway(width):
    return NEAR.get(width, -(-width // 256) * 128)


def steps(width):
    cut = halfway(width)
    return [
        (at, min(PIECE, end - at))
        for begin, end in ((0, cut), (cut, width))
        for at in range(begin, end, PIECE)
    ]


def relayed(members):
    return members == 8


def column_of(row):
    return jnp.broadcast_to(row, (128, row.shape[1])).T[:, 0:1]


def row_of(column):
    return jnp.broadcast_to(column, (column.shape[0], 128)).T[0:1]


def pack(doc, guide, offset, width, devices, capacity):
    rows, features = doc.shape
    slots = devices * capacity
    first = isinstance(guide, tuple)
    tail = META if first else 0
    pieces = steps(width)
    rest = [(at, min(PIECE, features - at)) for at in range(width, features, PIECE)] if first else []
    count = len(pieces)

    def kernel(*refs):
        if first:
            home_ref, exponent_ref, doc_ref, out_ref, order_ref, tile, packed, sems = refs
        else:
            order_ref, doc_ref, out_ref, tile, packed, sems = refs
        loads, stores = [], []
        for p, (at, wide) in enumerate(pieces + rest):
            loads.append(
                pltpu.make_async_copy(
                    doc_ref.at[:, pl.ds(offset + at, wide)], tile.at[:, pl.ds(at, wide)], sems.at[p]
                )
            )
            loads[-1].start()

        def send(begin, end):
            piece = pl.ds(begin, end - begin)
            stores.append(
                pltpu.make_async_copy(
                    packed.at[:, piece], out_ref.at[:, piece], sems.at[len(loads) + len(stores)]
                )
            )
            stores[-1].start()

        if first:
            home = home_ref[...].astype(F32)
            target = jnp.floor((home + 0.5) * (1.0 / rows))
            target_col = column_of(target)
            earlier = lax.broadcasted_iota(jnp.int32, (rows, rows), 0) < lax.broadcasted_iota(
                jnp.int32, (rows, rows), 1
            )
            rank = jnp.sum(
                jnp.where(earlier & (target_col == target), 1.0, 0.0), axis=0, keepdims=True
            )
            position = (target * capacity + rank).astype(jnp.int32)
            order = jnp.where(
                lax.broadcasted_iota(jnp.int32, (slots, rows), 0) == position, 1.0, 0.0
            ).astype(BF16)
            order_ref[...] = order
        else:
            order = order_ref[...]
        total = jnp.zeros((rows, 128), F32)
        for p, (at, wide) in enumerate(pieces):
            loads[p].wait()
            end = at + wide
            if first and p + 1 == count:
                for load in loads[count:]:
                    load.wait()
                end = features
            packed[:, at : at + wide] = jnp.dot(
                order, tile[:, at : at + wide], preferred_element_type=F32
            ).astype(BF16)
            if first:
                for column in range(at, end, 128):
                    values = tile[:, column : column + 128].astype(F32)
                    total = total + values * values
            send(at, at + wide)
        if first:
            square = row_of(jnp.sum(total, axis=1, keepdims=True))
            inverse = lax.rsqrt(square * (1.0 / features) + EPSILON)
            high = inverse.astype(BF16).astype(F32)
            middle = (inverse - high).astype(BF16).astype(F32)
            slot = home - target * rows
            slot_high = jnp.floor((slot + 0.5) * (1.0 / 32))
            field = lax.broadcasted_iota(jnp.int32, (META, rows), 0)
            meta = jnp.where(field == 0, 1.0, 0.0)
            for f, value in enumerate(
                (
                    slot_high,
                    slot - slot_high * 32,
                    exponent_ref[...].astype(F32),
                    high,
                    middle,
                    inverse - high - middle,
                ),
                1,
            ):
                meta = jnp.where(field == f, value, meta)
            packed[:, width:] = lax.dot_general(
                order, meta.astype(BF16), (((1,), (1,)), ((), ())), preferred_element_type=F32
            ).astype(BF16)
            send(width, width + META)
        for copy in stores:
            copy.wait()

    sent = jax.ShapeDtypeStruct((slots, width + tail), BF16)
    return pl.pallas_call(
        kernel,
        in_specs=[VM, VM, HBM] if first else [VM, HBM],
        out_specs=(HBM, VM) if first else HBM,
        out_shape=(sent, jax.ShapeDtypeStruct((slots, rows), BF16)) if first else sent,
        scratch_shapes=[
            pltpu.VMEM((rows, features if first else width), BF16),
            pltpu.VMEM((slots, width + tail), BF16),
            pltpu.SemaphoreType.DMA((2 * count + len(rest) + 1,)),
        ],
        compiler_params=WHOLE,
        name="pack_first" if first else "pack_next",
    )(*(guide if first else (guide,)), doc)


def unpack(got, order, rows):
    slots, width = got.shape
    first = order is None
    cut = halfway(width)

    def kernel(*refs):
        if first:
            got_ref, own_ref, near_ref, far_ref, order_ref, tile, placed, sems = refs
        else:
            got_ref, order_in, own_ref, near_ref, far_ref, tile, placed, order_ref, sems = refs
            given = pltpu.make_async_copy(order_in, order_ref, sems.at[0])
            given.start()
        begins = [width - META, 0] if first else [0]
        loads = []
        for n, begin in enumerate(begins):
            piece = pl.ds(begin, META if first and n == 0 else width - META * first)
            loads.append(
                pltpu.make_async_copy(got_ref.at[:, piece], tile.at[:, piece], sems.at[1 + n])
            )
            loads[-1].start()
        loads[0].wait()
        if first:
            fields = tile[:, width - META :].astype(F32)
            slot = fields[:, 1:2] * 32 + fields[:, 2:3]
            home = lax.broadcasted_iota(jnp.int32, (slots, rows), 1).astype(F32)
            hit = (home == slot) & (fields[:, 0:1] > 0.5)
            order_ref[...] = jnp.where(hit, 1.0, 0.0).T.astype(BF16)
            loads[1].wait()
        else:
            given.wait()
        stores = []
        for n, (begin, end, ref) in enumerate(((cut, width, far_ref), (0, cut, near_ref))):
            placed[:, begin:end] = jnp.dot(
                order_ref[...], tile[:, begin:end], preferred_element_type=F32
            ).astype(BF16)
            piece = pl.ds(begin, end - begin)
            for m, target in enumerate((ref, own_ref.at[:, piece])):
                stores.append(
                    pltpu.make_async_copy(placed.at[:, piece], target, sems.at[3 + 2 * n + m])
                )
                stores[-1].start()
        for copy in stores:
            copy.wait()

    outs = [jax.ShapeDtypeStruct((rows, columns), BF16) for columns in (width, cut, width - cut)]
    if first:
        outs.append(jax.ShapeDtypeStruct((rows, slots), BF16))
    result = pl.pallas_call(
        kernel,
        in_specs=[HBM] if first else [HBM, HBM],
        out_specs=[HBM] * 3 + [VM] * first,
        out_shape=outs,
        scratch_shapes=[pltpu.VMEM(got.shape, BF16), pltpu.VMEM((rows, width), BF16)]
        + [pltpu.VMEM((rows, slots), BF16)] * (not first)
        + [pltpu.SemaphoreType.DMA((7,))],
        compiler_params=WHOLE,
        name="unpack_first" if first else "unpack_next",
    )(*((got,) if first else (got, order)))
    return result[:3], result[3] if first else order


def runs(member_ref, cluster_ref):
    blocks = cluster_ref.shape[1]
    base = member_ref[0] * B_DEV

    def cluster(index):
        inside = (index >= 0) & (index < blocks)
        return jnp.where(inside, cluster_ref[0, jnp.clip(index, 0, blocks - 1)], -1)

    result = []
    for b in range(B_DEV):
        mine = cluster(base + b)
        back = jnp.where(
            cluster(base + b - 2) == mine, 2, jnp.where(cluster(base + b - 1) == mine, 1, 0)
        )
        links = [
            jnp.where(cluster(base + b - back + k) == mine, 1, 0) for k in range(RUN)
        ]
        result.append((back, links))
    return result


def load_window(member_ref, members, parts, window, sems, half):
    own, partner = parts[:2]
    rows, width = own.shape
    cut = halfway(width)
    member = member_ref[0]
    partner_at = pl.multiple_of((1 - member % 2) * 2 * rows, rows)
    other_at = pl.multiple_of((member % 2) * 2 * rows, rows)
    middle = (member == members // 2) | (member == members // 2 - 1)
    columns = pl.ds(half * cut, width - cut if half else cut)
    other = window.at[pl.ds(other_at, rows), columns]
    copies = [
        pltpu.make_async_copy(source, target, sems.at[3 * half + n])
        for n, (source, target) in enumerate(
            (
                (own.at[:, columns], window.at[pl.ds(rows, rows), columns]),
                (partner.at[:, columns], window.at[pl.ds(partner_at, rows), columns]),
                (parts[2 + half], other),
            )
        )
    ]
    copies[0].start()
    copies[1].start()
    if half == 0 or len(parts) == 4:
        copies[2].start()
    else:
        relay = pltpu.make_async_copy(parts[4], other, sems.at[3 * half + 2])
        pl.when(middle)(relay.start)
        pl.when(jnp.logical_not(middle))(copies[2].start)
    return copies


def run_scores(window, back, b, column, end):
    first = pl.multiple_of((SPAN + b - back) * BLK, BLK)
    return lax.dot_general(
        window[(SPAN + b) * BLK : (SPAN + b + 1) * BLK, column:end],
        window[pl.ds(first, RUN * BLK), column:end],
        (((1,), (1,)), ((), ())),
        preferred_element_type=F32,
    )


def partial_scores(member, members, cluster, parts, score):
    rows, width = parts[0].shape
    given = score is not None
    number = len(parts)

    def kernel(member_ref, cluster_ref, *refs):
        if given:
            score_in, score_ref, window, sems = refs[number:]
        else:
            score_ref, factor_ref, window, sems = refs[number:]
        found = runs(member_ref, cluster_ref)
        halves = [
            load_window(member_ref, members, refs[:number], window, sems, half) for half in (0, 1)
        ]
        for copy in halves[0] + halves[1]:
            copy.wait()
        for b in range(B_DEV):
            value = run_scores(window, found[b][0], b, 0, width if given else width - META)
            score_ref[b] = value + score_in[b] if given else value
        if not given:
            for side in range(3):
                fields = window[side * rows : (side + 1) * rows, width - META :].astype(F32).T
                field = lax.broadcasted_iota(jnp.int32, (8, rows), 0)
                inverse = fields[4:5] + fields[5:6] + fields[6:7]
                factor_ref[side] = jnp.where(field == 0, inverse, jnp.exp2(fields[3:4]))

    score_shape = jax.ShapeDtypeStruct((B_DEV, BLK, RUN * BLK), F32)
    return pl.pallas_call(
        kernel,
        in_specs=[SM, SM] + [HBM] * number + [VM] * given,
        out_shape=score_shape if given else (score_shape, jax.ShapeDtypeStruct((3, 8, rows), F32)),
        scratch_shapes=[
            pltpu.VMEM((3 * rows, width), BF16),
            pltpu.SemaphoreType.DMA((6,)),
        ],
        compiler_params=WHOLE,
        name="partial_scores",
    )(member, cluster, *parts, *([score] if given else []))


def finish(member, members, cluster, chunks, score, factor, features):
    rows = chunks[0][0].shape[0]
    count = len(chunks)
    widths = [chunk[0].shape[1] for chunk in chunks]
    number = len(chunks[0])
    last = count - 1

    def kernel(member_ref, cluster_ref, *refs):
        parts = [refs[number * c : number * (c + 1)] for c in range(count)]
        score_in, factor_in, out_ref, log_ref = refs[number * count : number * count + 4]
        packed, value_ref, factor_ref, early_sems, out_sems, load_sems = refs[
            number * count + 4 : number * count + 10
        ]
        windows = refs[number * count + 10 :]
        found = runs(member_ref, cluster_ref)
        loads = {}

        def load(c, half):
            copies = load_window(member_ref, members, parts[c], windows[c], load_sems.at[c], half)
            loads.setdefault(c, []).append(copies)

        load(last, 0)
        early = [
            pltpu.make_async_copy(score_in, value_ref, early_sems.at[0]),
            pltpu.make_async_copy(factor_in, factor_ref, early_sems.at[1]),
        ]
        for copy in early:
            copy.start()
        load(last, 1)
        cut = halfway(widths[last])
        for half, (column, end) in enumerate(((0, cut), (cut, widths[last]))):
            for copy in loads[last][half] + (early if half == 0 else []):
                copy.wait()
            for c in reversed(range(last)):
                if (c == last - 1) == (half == 0):
                    load(c, 0)
                    load(c, 1)
            for b in range(B_DEV):
                value_ref[b] += run_scores(windows[last], found[b][0], b, column, end)
        apart = lax.broadcasted_iota(jnp.int32, (BLK, BLK), 0) - lax.broadcasted_iota(
            jnp.int32, (BLK, BLK), 1
        )
        weights = []
        for b in range(B_DEV):
            back, links = found[b]
            mine = factor_ref[1, :, b * BLK : (b + 1) * BLK]
            row_scale = column_of(mine[0:1]) * features**-0.5
            density = jnp.zeros((BLK, 1), F32)
            tiles = []
            for k in range(RUN):
                block = SPAN + b - back + k
                far = factor_ref[block // B_DEV, :, pl.ds(pl.multiple_of((block % B_DEV) * BLK, BLK), BLK)]
                value = jnp.exp(
                    value_ref[b, :, k * BLK : (k + 1) * BLK] * row_scale * far[0:1] - KERNEL_SHIFT
                )
                kept = (apart + jnp.where(back == k, 0, 2 * BLK) != 0) & (
                    jnp.full((BLK, BLK), links[k], jnp.int32) > 0
                )
                value = jnp.where(kept, value, 0.0)
                density = density + jnp.sum(value, axis=1, keepdims=True)
                tiles.append((value.astype(BF16).astype(F32) * far[1:2]).astype(BF16))
            weights.append(jnp.concatenate(tiles, axis=1))
            log_ref[:, b * BLK : (b + 1) * BLK] = jnp.log(row_of(density))
        outgoing = []
        for c in reversed(range(count)):
            if c != last:
                for copy in loads[c][0] + loads[c][1]:
                    copy.wait()
            out_at = sum(CHUNKS[:c])
            for at, wide in steps(CHUNKS[c]):
                for b in range(B_DEV):
                    first = pl.multiple_of((SPAN + b - found[b][0]) * BLK, BLK)
                    packed[b * BLK : (b + 1) * BLK, out_at + at : out_at + at + wide] = jnp.dot(
                        weights[b],
                        windows[c][pl.ds(first, RUN * BLK), at : at + wide],
                        preferred_element_type=F32,
                    ).astype(BF16)
                piece = pl.ds(out_at + at, wide)
                copy = pltpu.make_async_copy(
                    packed.at[:, piece], out_ref.at[:, piece], out_sems.at[len(outgoing)]
                )
                copy.start()
                outgoing.append(copy)
        for copy in outgoing:
            copy.wait()

    flat = [ref for chunk in chunks for ref in chunk]
    return pl.pallas_call(
        kernel,
        in_specs=[SM, SM] + [HBM] * (len(flat) + 2),
        out_specs=(HBM, VM),
        out_shape=(
            jax.ShapeDtypeStruct((rows, features), BF16),
            jax.ShapeDtypeStruct((1, rows), F32),
        ),
        scratch_shapes=[
            pltpu.VMEM((rows, features), BF16),
            pltpu.VMEM((B_DEV, BLK, RUN * BLK), F32),
            pltpu.VMEM((3, 8, rows), F32),
            pltpu.SemaphoreType.DMA((2,)),
            pltpu.SemaphoreType.DMA((sum(len(steps(width)) for width in CHUNKS),)),
            pltpu.SemaphoreType.DMA((count, 6)),
        ]
        + [pltpu.VMEM((3 * rows, width), BF16) for width in widths],
        compiler_params=WHOLE,
        name="finish",
    )(member, cluster, *flat, score, factor)


def neighbours(own, near, far, members, beside):
    middle = members // 2
    odd = range(1, members - 1, 2)
    hops = [(i, i + 1) for i in odd] + [(i + 1, i) for i in odd]
    around = [(middle - 1, members - 1), (middle, 0)]
    onward = [(members - 1, middle), (0, middle - 1)]
    apart = [hop for hop in hops if set(hop) != {middle - 1, middle}]
    far = lax.ppermute(far, "member", apart + around if relayed(members) else hops)
    near = lax.ppermute(near, "member", hops)
    partner = lax.ppermute(own, "member", [(i, i ^ 1) for i in range(members)])
    if relayed(members):
        first = far
        if beside:
            first, _ = lax.optimization_barrier((far, partner))
        return (own, partner, near, far, lax.ppermute(first, "member", onward))
    return (own, partner, near, far)


def body(doc_mantissa, doc_exponent, doc_home, block_cluster):
    rows, features = doc_mantissa.shape
    members = lax.axis_size("member")
    devices = lax.axis_size("group") * members
    capacity = rows // devices * 3 // 2
    member = lax.axis_index("member").reshape(1)
    sends = []
    guide = (doc_home[None, :], doc_exponent[None, :])
    for c, width in enumerate(CHUNKS):
        sent = pack(doc_mantissa, guide, sum(CHUNKS[:c]), width, devices, capacity)
        if c == 0:
            sent, guide = sent
        sends.append(sent)

    chunks = []
    order = score = factor = None

    def scored(c, score):
        found = partial_scores(member, members, block_cluster, chunks[c], score)
        return found if c == 0 else (found, factor)

    for c in range(len(CHUNKS)):
        if c > 1:
            sends[c], _ = lax.optimization_barrier((sends[c], chunks[c - 2]))
            score, factor = scored(c - 2, score)
        got = lax.all_to_all(
            sends[c].reshape(devices, capacity, -1), ("group", "member"), 0, 0, tiled=True
        ).reshape(devices * capacity, -1)
        if c > 0:
            got, *_ = lax.optimization_barrier((got, chunks[-1], score))
        parts, order = unpack(got, order, rows)
        chunks.append(neighbours(*parts, members, c + 1 < len(CHUNKS)))
    score, factor = scored(len(CHUNKS) - 2, score)
    embed_sum, log_density = finish(
        member, members, block_cluster, chunks, score, factor, features
    )
    return embed_sum, log_density.reshape(rows)


def solution(mesh):
    return jax.shard_map(
        body,
        mesh=mesh,
        in_specs=(
            P(("group", "member"), None),
            P(("group", "member")),
            P(("group", "member")),
            P("group", None),
        ),
        out_specs=(P(("group", "member"), None), P(("group", "member"))),
        check_vma=False,
    )
```

```python
import jax
import jax.numpy as jnp
from jax import lax
from jax.experimental import pallas as pl
from jax.experimental.pallas import tpu as pltpu
from jax.sharding import PartitionSpec as P

BLK = 256
B_DEV = 2
SPAN = 2
RUN = SPAN + 1
WINDOW = B_DEV + 2 * SPAN
META = 128
KERNEL_SHIFT = 4.0
EPSILON = 1e-06
CHUNKS = (1280, 1536, 1280)
PIECE = 896
NEAR = {CHUNKS[1]: 896}

F32 = jnp.float32
BF16 = jnp.bfloat16
VM = pl.BlockSpec(memory_space=pltpu.VMEM)
SM = pl.BlockSpec(memory_space=pltpu.SMEM)
HBM = pl.BlockSpec(memory_space=pltpu.HBM)
WHOLE = pltpu.CompilerParams(vmem_limit_bytes=64 * 1024 * 1024)


def halfway(width):
    return NEAR.get(width, -(-width // 256) * 128)


def steps(width):
    cut = halfway(width)
    return [
        (at, min(PIECE, end - at))
        for begin, end in ((0, cut), (cut, width))
        for at in range(begin, end, PIECE)
    ]


def relayed(members):
    return members == 8


def column_of(row):
    return jnp.broadcast_to(row, (128, row.shape[1])).T[:, 0:1]


def row_of(column):
    return jnp.broadcast_to(column, (column.shape[0], 128)).T[0:1]


def pack(doc, guide, offset, width, devices, capacity):
    rows, features = doc.shape
    slots = devices * capacity
    first = isinstance(guide, tuple)
    tail = META if first else 0
    pieces = steps(width)
    rest = [(at, min(PIECE, features - at)) for at in range(width, features, PIECE)] if first else []
    count = len(pieces)

    def kernel(*refs):
        if first:
            home_ref, exponent_ref, doc_ref, out_ref, order_ref, tile, packed, sems = refs
        else:
            order_ref, doc_ref, out_ref, tile, packed, sems = refs
        loads, stores = [], []
        for p, (at, wide) in enumerate(pieces + rest):
            loads.append(
                pltpu.make_async_copy(
                    doc_ref.at[:, pl.ds(offset + at, wide)], tile.at[:, pl.ds(at, wide)], sems.at[p]
                )
            )
            loads[-1].start()

        def send(begin, end):
            piece = pl.ds(begin, end - begin)
            stores.append(
                pltpu.make_async_copy(
                    packed.at[:, piece], out_ref.at[:, piece], sems.at[len(loads) + len(stores)]
                )
            )
            stores[-1].start()

        if first:
            home = home_ref[...].astype(F32)
            target = jnp.floor((home + 0.5) * (1.0 / rows))
            target_col = column_of(target)
            earlier = lax.broadcasted_iota(jnp.int32, (rows, rows), 0) < lax.broadcasted_iota(
                jnp.int32, (rows, rows), 1
            )
            rank = jnp.sum(
                jnp.where(earlier & (target_col == target), 1.0, 0.0), axis=0, keepdims=True
            )
            position = (target * capacity + rank).astype(jnp.int32)
            order = jnp.where(
                lax.broadcasted_iota(jnp.int32, (slots, rows), 0) == position, 1.0, 0.0
            ).astype(BF16)
            order_ref[...] = order
        else:
            order = order_ref[...]
        total = jnp.zeros((rows, 128), F32)
        for p, (at, wide) in enumerate(pieces):
            loads[p].wait()
            end = at + wide
            if first and p + 1 == count:
                for load in loads[count:]:
                    load.wait()
                end = features
            packed[:, at : at + wide] = jnp.dot(
                order, tile[:, at : at + wide], preferred_element_type=F32
            ).astype(BF16)
            if first:
                for column in range(at, end, 128):
                    values = tile[:, column : column + 128].astype(F32)
                    total = total + values * values
            send(at, at + wide)
        if first:
            square = row_of(jnp.sum(total, axis=1, keepdims=True))
            inverse = lax.rsqrt(square * (1.0 / features) + EPSILON)
            high = inverse.astype(BF16).astype(F32)
            middle = (inverse - high).astype(BF16).astype(F32)
            slot = home - target * rows
            slot_high = jnp.floor((slot + 0.5) * (1.0 / 32))
            field = lax.broadcasted_iota(jnp.int32, (META, rows), 0)
            meta = jnp.where(field == 0, 1.0, 0.0)
            for f, value in enumerate(
                (
                    slot_high,
                    slot - slot_high * 32,
                    exponent_ref[...].astype(F32),
                    high,
                    middle,
                    inverse - high - middle,
                ),
                1,
            ):
                meta = jnp.where(field == f, value, meta)
            packed[:, width:] = lax.dot_general(
                order, meta.astype(BF16), (((1,), (1,)), ((), ())), preferred_element_type=F32
            ).astype(BF16)
            send(width, width + META)
        for copy in stores:
            copy.wait()

    sent = jax.ShapeDtypeStruct((slots, width + tail), BF16)
    return pl.pallas_call(
        kernel,
        in_specs=[VM, VM, HBM] if first else [VM, HBM],
        out_specs=(HBM, VM) if first else HBM,
        out_shape=(sent, jax.ShapeDtypeStruct((slots, rows), BF16)) if first else sent,
        scratch_shapes=[
            pltpu.VMEM((rows, features if first else width), BF16),
            pltpu.VMEM((slots, width + tail), BF16),
            pltpu.SemaphoreType.DMA((2 * count + len(rest) + 1,)),
        ],
        compiler_params=WHOLE,
        name="pack_first" if first else "pack_next",
    )(*(guide if first else (guide,)), doc)


def unpack(got, order, rows):
    slots, width = got.shape
    first = order is None
    cut = halfway(width)

    def kernel(*refs):
        if first:
            got_ref, own_ref, near_ref, far_ref, order_ref, tile, placed, sems = refs
        else:
            got_ref, order_in, own_ref, near_ref, far_ref, tile, placed, order_ref, sems = refs
            given = pltpu.make_async_copy(order_in, order_ref, sems.at[0])
            given.start()
        begins = [width - META, 0] if first else [0]
        loads = []
        for n, begin in enumerate(begins):
            piece = pl.ds(begin, META if first and n == 0 else width - META * first)
            loads.append(
                pltpu.make_async_copy(got_ref.at[:, piece], tile.at[:, piece], sems.at[1 + n])
            )
            loads[-1].start()
        loads[0].wait()
        if first:
            fields = tile[:, width - META :].astype(F32)
            slot = fields[:, 1:2] * 32 + fields[:, 2:3]
            home = lax.broadcasted_iota(jnp.int32, (slots, rows), 1).astype(F32)
            hit = (home == slot) & (fields[:, 0:1] > 0.5)
            order_ref[...] = jnp.where(hit, 1.0, 0.0).T.astype(BF16)
            loads[1].wait()
        else:
            given.wait()
        stores = []
        for n, (begin, end, ref) in enumerate(((cut, width, far_ref), (0, cut, near_ref))):
            placed[:, begin:end] = jnp.dot(
                order_ref[...], tile[:, begin:end], preferred_element_type=F32
            ).astype(BF16)
            piece = pl.ds(begin, end - begin)
            for m, target in enumerate((ref, own_ref.at[:, piece])):
                stores.append(
                    pltpu.make_async_copy(placed.at[:, piece], target, sems.at[3 + 2 * n + m])
                )
                stores[-1].start()
        for copy in stores:
            copy.wait()

    outs = [jax.ShapeDtypeStruct((rows, columns), BF16) for columns in (width, cut, width - cut)]
    if first:
        outs.append(jax.ShapeDtypeStruct((rows, slots), BF16))
    result = pl.pallas_call(
        kernel,
        in_specs=[HBM] if first else [HBM, HBM],
        out_specs=[HBM] * 3 + [VM] * first,
        out_shape=outs,
        scratch_shapes=[pltpu.VMEM(got.shape, BF16), pltpu.VMEM((rows, width), BF16)]
        + [pltpu.VMEM((rows, slots), BF16)] * (not first)
        + [pltpu.SemaphoreType.DMA((7,))],
        compiler_params=WHOLE,
        name="unpack_first" if first else "unpack_next",
    )(*((got,) if first else (got, order)))
    return result[:3], result[3] if first else order


def runs(member_ref, cluster_ref):
    blocks = cluster_ref.shape[1]
    base = member_ref[0] * B_DEV

    def cluster(index):
        inside = (index >= 0) & (index < blocks)
        return jnp.where(inside, cluster_ref[0, jnp.clip(index, 0, blocks - 1)], -1)

    result = []
    for b in range(B_DEV):
        mine = cluster(base + b)
        back = jnp.where(
            cluster(base + b - 2) == mine, 2, jnp.where(cluster(base + b - 1) == mine, 1, 0)
        )
        links = [
            jnp.where(cluster(base + b - back + k) == mine, 1, 0) for k in range(RUN)
        ]
        result.append((back, links))
    return result


def load_window(member_ref, members, parts, window, sems, half):
    own, partner = parts[:2]
    rows, width = own.shape
    cut = halfway(width)
    member = member_ref[0]
    partner_at = pl.multiple_of((1 - member % 2) * 2 * rows, rows)
    other_at = pl.multiple_of((member % 2) * 2 * rows, rows)
    middle = (member == members // 2) | (member == members // 2 - 1)
    columns = pl.ds(half * cut, width - cut if half else cut)
    other = window.at[pl.ds(other_at, rows), columns]
    copies = [
        pltpu.make_async_copy(source, target, sems.at[3 * half + n])
        for n, (source, target) in enumerate(
            (
                (own.at[:, columns], window.at[pl.ds(rows, rows), columns]),
                (partner.at[:, columns], window.at[pl.ds(partner_at, rows), columns]),
                (parts[2 + half], other),
            )
        )
    ]
    copies[0].start()
    copies[1].start()
    if half == 0 or len(parts) == 4:
        copies[2].start()
    else:
        relay = pltpu.make_async_copy(parts[4], other, sems.at[3 * half + 2])
        pl.when(middle)(relay.start)
        pl.when(jnp.logical_not(middle))(copies[2].start)
    return copies


def run_scores(window, back, b, column, end):
    first = pl.multiple_of((SPAN + b - back) * BLK, BLK)
    return lax.dot_general(
        window[(SPAN + b) * BLK : (SPAN + b + 1) * BLK, column:end],
        window[pl.ds(first, RUN * BLK), column:end],
        (((1,), (1,)), ((), ())),
        preferred_element_type=F32,
    )


def partial_scores(member, members, cluster, parts, score):
    rows, width = parts[0].shape
    given = score is not None
    number = len(parts)

    def kernel(member_ref, cluster_ref, *refs):
        if given:
            score_in, score_ref, window, sems = refs[number:]
        else:
            score_ref, factor_ref, window, sems = refs[number:]
        found = runs(member_ref, cluster_ref)
        halves = [
            load_window(member_ref, members, refs[:number], window, sems, half) for half in (0, 1)
        ]
        for copy in halves[0] + halves[1]:
            copy.wait()
        for b in range(B_DEV):
            value = run_scores(window, found[b][0], b, 0, width if given else width - META)
            score_ref[b] = value + score_in[b] if given else value
        if not given:
            for side in range(3):
                fields = window[side * rows : (side + 1) * rows, width - META :].astype(F32).T
                field = lax.broadcasted_iota(jnp.int32, (8, rows), 0)
                inverse = fields[4:5] + fields[5:6] + fields[6:7]
                factor_ref[side] = jnp.where(field == 0, inverse, jnp.exp2(fields[3:4]))

    score_shape = jax.ShapeDtypeStruct((B_DEV, BLK, RUN * BLK), F32)
    return pl.pallas_call(
        kernel,
        in_specs=[SM, SM] + [HBM] * number + [VM] * given,
        out_shape=score_shape if given else (score_shape, jax.ShapeDtypeStruct((3, 8, rows), F32)),
        scratch_shapes=[
            pltpu.VMEM((3 * rows, width), BF16),
            pltpu.SemaphoreType.DMA((6,)),
        ],
        compiler_params=WHOLE,
        name="partial_scores",
    )(member, cluster, *parts, *([score] if given else []))


def finish(member, members, cluster, chunks, score, factor, features):
    rows = chunks[0][0].shape[0]
    count = len(chunks)
    widths = [chunk[0].shape[1] for chunk in chunks]
    number = len(chunks[0])
    last = count - 1

    def kernel(member_ref, cluster_ref, *refs):
        parts = [refs[number * c : number * (c + 1)] for c in range(count)]
        score_in, factor_in, out_ref, log_ref = refs[number * count : number * count + 4]
        packed, value_ref, factor_ref, early_sems, out_sems, load_sems = refs[
            number * count + 4 : number * count + 10
        ]
        windows = refs[number * count + 10 :]
        found = runs(member_ref, cluster_ref)
        loads = {}

        def load(c, half):
            copies = load_window(member_ref, members, parts[c], windows[c], load_sems.at[c], half)
            loads.setdefault(c, []).append(copies)

        load(last, 0)
        early = [
            pltpu.make_async_copy(score_in, value_ref, early_sems.at[0]),
            pltpu.make_async_copy(factor_in, factor_ref, early_sems.at[1]),
        ]
        for copy in early:
            copy.start()
        load(last, 1)
        cut = halfway(widths[last])
        for half, (column, end) in enumerate(((0, cut), (cut, widths[last]))):
            for copy in loads[last][half] + (early if half == 0 else []):
                copy.wait()
            for c in reversed(range(last)):
                if (c == last - 1) == (half == 0):
                    load(c, 0)
                    load(c, 1)
            for b in range(B_DEV):
                value_ref[b] += run_scores(windows[last], found[b][0], b, column, end)
        apart = lax.broadcasted_iota(jnp.int32, (BLK, BLK), 0) - lax.broadcasted_iota(
            jnp.int32, (BLK, BLK), 1
        )
        weights = []
        for b in range(B_DEV):
            back, links = found[b]
            mine = factor_ref[1, :, b * BLK : (b + 1) * BLK]
            row_scale = column_of(mine[0:1]) * features**-0.5
            density = jnp.zeros((BLK, 1), F32)
            tiles = []
            for k in range(RUN):
                block = SPAN + b - back + k
                far = factor_ref[block // B_DEV, :, pl.ds(pl.multiple_of((block % B_DEV) * BLK, BLK), BLK)]
                value = jnp.exp(
                    value_ref[b, :, k * BLK : (k + 1) * BLK] * row_scale * far[0:1] - KERNEL_SHIFT
                )
                kept = (apart + jnp.where(back == k, 0, 2 * BLK) != 0) & (
                    jnp.full((BLK, BLK), links[k], jnp.int32) > 0
                )
                value = jnp.where(kept, value, 0.0)
                density = density + jnp.sum(value, axis=1, keepdims=True)
                tiles.append((value.astype(BF16).astype(F32) * far[1:2]).astype(BF16))
            weights.append(jnp.concatenate(tiles, axis=1))
            log_ref[:, b * BLK : (b + 1) * BLK] = jnp.log(row_of(density))
        outgoing = []
        for c in reversed(range(count)):
            if c != last:
                for copy in loads[c][0] + loads[c][1]:
                    copy.wait()
            out_at = sum(CHUNKS[:c])
            for at, wide in steps(CHUNKS[c]):
                for b in range(B_DEV):
                    first = pl.multiple_of((SPAN + b - found[b][0]) * BLK, BLK)
                    packed[b * BLK : (b + 1) * BLK, out_at + at : out_at + at + wide] = jnp.dot(
                        weights[b],
                        windows[c][pl.ds(first, RUN * BLK), at : at + wide],
                        preferred_element_type=F32,
                    ).astype(BF16)
                piece = pl.ds(out_at + at, wide)
                copy = pltpu.make_async_copy(
                    packed.at[:, piece], out_ref.at[:, piece], out_sems.at[len(outgoing)]
                )
                copy.start()
                outgoing.append(copy)
        for copy in outgoing:
            copy.wait()

    flat = [ref for chunk in chunks for ref in chunk]
    return pl.pallas_call(
        kernel,
        in_specs=[SM, SM] + [HBM] * (len(flat) + 2),
        out_specs=(HBM, VM),
        out_shape=(
            jax.ShapeDtypeStruct((rows, features), BF16),
            jax.ShapeDtypeStruct((1, rows), F32),
        ),
        scratch_shapes=[
            pltpu.VMEM((rows, features), BF16),
            pltpu.VMEM((B_DEV, BLK, RUN * BLK), F32),
            pltpu.VMEM((3, 8, rows), F32),
            pltpu.SemaphoreType.DMA((2,)),
            pltpu.SemaphoreType.DMA((sum(len(steps(width)) for width in CHUNKS),)),
            pltpu.SemaphoreType.DMA((count, 6)),
        ]
        + [pltpu.VMEM((3 * rows, width), BF16) for width in widths],
        compiler_params=WHOLE,
        name="finish",
    )(member, cluster, *flat, score, factor)


def neighbours(own, near, far, members, beside):
    middle = members // 2
    odd = range(1, members - 1, 2)
    hops = [(i, i + 1) for i in odd] + [(i + 1, i) for i in odd]
    around = [(middle - 1, members - 1), (middle, 0)]
    onward = [(members - 1, middle), (0, middle - 1)]
    apart = [hop for hop in hops if set(hop) != {middle - 1, middle}]
    far = lax.ppermute(far, "member", apart + around if relayed(members) else hops)
    near = lax.ppermute(near, "member", hops)
    partner = lax.ppermute(own, "member", [(i, i ^ 1) for i in range(members)])
    if relayed(members):
        first = far
        if beside:
            first, _ = lax.optimization_barrier((far, partner))
        return (own, partner, near, far, lax.ppermute(first, "member", onward))
    return (own, partner, near, far)


def body(doc_mantissa, doc_exponent, doc_home, block_cluster):
    rows, features = doc_mantissa.shape
    members = lax.axis_size("member")
    devices = lax.axis_size("group") * members
    capacity = rows // devices * 3 // 2
    member = lax.axis_index("member").reshape(1)
    sends = []
    guide = (doc_home[None, :], doc_exponent[None, :])
    for c, width in enumerate(CHUNKS):
        sent = pack(doc_mantissa, guide, sum(CHUNKS[:c]), width, devices, capacity)
        if c == 0:
            sent, guide = sent
        sends.append(sent)

    chunks = []
    order = score = factor = None

    def scored(c, score):
        found = partial_scores(member, members, block_cluster, chunks[c], score)
        return found if c == 0 else (found, factor)

    for c in range(len(CHUNKS)):
        if c > 1:
            sends[c], _ = lax.optimization_barrier((sends[c], chunks[c - 2]))
            score, factor = scored(c - 2, score)
        got = lax.all_to_all(
            sends[c].reshape(devices, capacity, -1), ("group", "member"), 0, 0, tiled=True
        ).reshape(devices * capacity, -1)
        if c > 0:
            got, *_ = lax.optimization_barrier((got, chunks[-1], score))
        parts, order = unpack(got, order, rows)
        chunks.append(neighbours(*parts, members, c + 1 < len(CHUNKS)))
    score, factor = scored(len(CHUNKS) - 2, score)
    embed_sum, log_density = finish(
        member, members, block_cluster, chunks, score, factor, features
    )
    return embed_sum, log_density.reshape(rows)


def solution(mesh):
    return jax.shard_map(
        body,
        mesh=mesh,
        in_specs=(
            P(("group", "member"), None),
            P(("group", "member")),
            P(("group", "member")),
            P("group", None),
        ),
        out_specs=(P(("group", "member"), None), P(("group", "member"))),
        check_vma=False,
    )
```
